256 devices in a mesh: rows: 32 (over x, z), centers: 8 (over y, core).
Axes of the slice: x: 4, y: 4, z: 8, core: 2. Of those that a mesh axis runs over, the one named last changes fastest.
Arguments:
- features: bfloat16 [440, 32768], P(None, 'rows'), may hold values from -16 to 16
- labels: int32 [32768], P('rows'), may hold values from 0 to 146
- center_index: int32 [8, 2048], P('centers'), may hold values from 0 to 32767
- warm_coef: float32 [147, 16384], P(None, 'centers'), may hold values from -10 to 10
Outputs:
- coef_out: float32 [147, 16384], P(None, 'centers')
- logits_out: float32 [147, 32768], P(None, ('rows', 'centers'))
The draws below stay inside these ranges and needn't reach their ends.
All inputs are finite; a program needn't handle non-finite values.
Results may differ from the reference program's by a relative error of at most 0.0067.
Values may be sent and summed in bfloat16 or wider, within the bound.
No kernel may reach another device: no remote copies, remote signals or barrier semaphores. Data moves between devices by JAX's collectives and lax.ppermute only.
A program may use at most 64 MiB of HBM per device.

```python
import math
import jax
import jax.numpy as jnp
from jax import lax

F = 440
C = 147
CENTERS = 2048
ROUNDS = 2
PASSES = 2
GROUPS = 8
ROWS = 32768


def draw_features(key, part):
    key_mix = jax.random.fold_in(key, 101)
    key_lat = jax.random.fold_in(key, 202)
    key_jitter = jax.random.fold_in(key, 303)
    latent_dim = 6
    spread = 1.65
    mixing = jax.random.normal(key_mix, (F, latent_dim), jnp.float32)
    latent = jax.random.normal(key_lat, (latent_dim, ROWS), jnp.float32)
    jitter = 0.6 * jax.random.normal(key_jitter, (F, ROWS), jnp.float32)
    values = math.sqrt(spread) * jnp.dot(mixing, latent, precision=lax.Precision.HIGHEST) + jitter
    return jnp.clip(values, -16.0, 16.0).astype(jnp.bfloat16)


def place_ends(values, stream_key, smallest, high):
    longest = values.shape.index(max(values.shape))
    spots = []
    for shift in (0, 1):
        where = [jax.random.randint(jax.random.fold_in(stream_key, axis), (), 0, length) for axis, length in enumerate(values.shape)]
        where[longest] = (where[longest] + shift) % values.shape[longest]
        spots.append(tuple(where))
    return values.at[spots[0]].set(smallest).at[spots[1]].set(high)


def level_of(stream_key, dims, split, least, high):
    factor_of = 1.0
    for position, parts in split:
        steps = jax.random.uniform(jax.random.fold_in(jax.random.fold_in(stream_key, 6), position), (parts,), jnp.float32, least / len(split), high / len(split))
        factor_of = factor_of * jnp.repeat(jnp.exp(steps), dims[position] // parts).reshape((-1,) + (1,) * (len(dims) - 1 - position))
    return factor_of


def scatter_about(rng, extent, deviation, limit, pieces=(), kind=jnp.bfloat16):
    drawn = jax.random.normal(rng, extent, jnp.float32) * deviation
    if len(pieces) > 0:
        drawn = level_of(rng, extent, pieces, -0.22, 0.18) * drawn
    return jnp.clip(drawn, min=-limit, max=limit).astype(kind)


def setup_inputs(seed: int = 0) -> dict:
    arg_keys = jax.random.split(jax.random.key(seed), 5)
    features = draw_features(jax.random.fold_in(arg_keys[4], 71), 0)
    labels = place_ends(jax.random.randint(arg_keys[1], (ROWS,), 0, C), jax.random.fold_in(arg_keys[1], 1), 0, C - 1).astype(jnp.int32)
    center_index = place_ends(jax.random.randint(arg_keys[2], (GROUPS, CENTERS), 0, ROWS), jax.random.fold_in(arg_keys[2], 1), 0, ROWS - 1).astype(jnp.int32)
    warm_coef = scatter_about(arg_keys[3], (C, GROUPS * CENTERS), 2.0, 10.0, ((1, 8),), jnp.float32)
    return dict(features=features, labels=labels, center_index=center_index, warm_coef=warm_coef)


step_size = 0.1


def gauss_tile(features, row_norms, index_row):
    chosen = jnp.take(features, index_row.astype(jnp.int32), axis=1)
    center_norms = jnp.sum(jnp.square(chosen.astype(jnp.float32)), axis=0)
    cross_term = lax.dot_general(chosen, features, (((0,), (0,)), ((), ())), preferred_element_type=jnp.float32)
    dist_sq = center_norms[:, None] + row_norms[None, :] - 2.0 * cross_term
    return jnp.exp(-dist_sq / F).astype(jnp.bfloat16)


def reference(features, labels, center_index, warm_coef):
    row_norms = jnp.sum(jnp.square(features.astype(jnp.float32)), axis=0)
    one_hot = (labels[None, :] == jnp.arange(C, dtype=jnp.int32)[:, None]).astype(jnp.float32)
    weights = warm_coef.reshape(C, GROUPS, CENTERS).transpose(1, 0, 2)

    def first_scores(carry, pair):
        index_row, group_coef = pair
        kernel = gauss_tile(features, row_norms, index_row)
        return carry, jnp.dot(group_coef.astype(jnp.bfloat16), kernel, preferred_element_type=jnp.float32)

    _, own_parts = lax.scan(first_scores, jnp.float32(0.0), (center_index, weights))
    for round_idx in range(ROUNDS):
        summed = jnp.sum(own_parts, axis=0)

        def sweep(carry, trio):
            index_row, group_coef, own_part = trio
            kernel = gauss_tile(features, row_norms, index_row)
            base_part = summed - own_part
            group_part = own_part
            for pass_idx in range(PASSES):
                if pass_idx > 0:
                    group_part = jnp.dot(group_coef.astype(jnp.bfloat16), kernel, preferred_element_type=jnp.float32)
                logits = base_part + group_part
                raised = jnp.exp(logits)
                class_prob = raised / jnp.sum(raised, axis=0, keepdims=True)
                residual = (class_prob - one_hot).astype(jnp.bfloat16)
                gradient = lax.dot_general(residual, kernel, (((1,), (1,)), ((), ())), preferred_element_type=jnp.float32)
                group_coef = group_coef - step_size * gradient
            fresh = jnp.dot(group_coef.astype(jnp.bfloat16), kernel, preferred_element_type=jnp.float32)
            return carry, (group_coef, fresh)

        _, (weights, own_parts) = lax.scan(sweep, jnp.float32(0.0), (center_index, weights, own_parts))
    logits_out = jnp.sum(own_parts, axis=0)
    coef_out = weights.transpose(1, 0, 2).reshape(C, GROUPS * CENTERS)
    return coef_out, logits_out
```

```python
import jax
import jax.numpy as jnp
from jax import lax
from jax.experimental import pallas as pl
from jax.experimental.pallas import tpu as pltpu
from jax.sharding import PartitionSpec as P

ROUNDS = 2
PASSES = 2
STEP = 0.1

X, Z, Y, CORES = 4, 8, 4, 2
CLASSES = 147
PAD = 160
WIRE = 152
FEAT = 440
FPAD = 448
LANES = 128
CHUNK = X * LANES
PART = CHUNK // 4
BLOCK = 256

F32 = jnp.float32
BF16 = jnp.bfloat16
LOG2E = 1.4426950408889634

X_GROUPS = [[x * Z + z for x in range(X)] for z in range(Z)]
Z_GROUPS = [[x * Z + z for z in range(Z)] for x in range(X)]
Y_GROUPS = [[y * CORES + k for y in range(Y)] for k in range(CORES)]
CORE_SWAP = [(y * CORES + k, y * CORES + 1 - k) for y in range(Y) for k in range(CORES)]


def x_shift(d):
    return [(x * Z + z, (x + d) % X * Z + z) for x in range(X) for z in range(Z)]


def call(kernel, outs, scratch=(), name=None):
    vmem = pl.BlockSpec(memory_space=pltpu.VMEM)
    many = isinstance(outs, (list, tuple))
    return lambda *args: pl.pallas_call(
        kernel,
        out_shape=outs,
        in_specs=[vmem] * len(args),
        out_specs=[vmem] * len(outs) if many else vmem,
        scratch_shapes=list(scratch),
        name=name,
    )(*args)


def like(shape, dtype):
    return jax.ShapeDtypeStruct(shape, dtype)


def my_x():
    return lax.axis_index("rows") // Z


def my_core():
    return lax.rem(lax.axis_index("centers"), CORES)


def chunk_of(d):
    return lax.rem(my_x() + X - d, X)


def spot(z, rows):
    top, left = z // 4 * rows, z % 4 * PART
    return slice(top, top + rows), left


def dot(a, b):
    return jnp.dot(a, b, preferred_element_type=F32)


def dot_nt(a, b):
    return lax.dot_general(a, b, (((1,), (1,)), ((), ())), preferred_element_type=F32)


def select_kernel(feat_ref, index_ref, out_ref):
    rows = feat_ref.shape[1]
    first = lax.axis_index("rows") * rows
    half = FPAD // 2

    @pl.loop(0, X)
    def _(c):
        wanted = index_ref[:, pl.ds(pl.multiple_of(c * CHUNK, CHUNK), CHUNK)] - first
        hot = lax.broadcasted_iota(jnp.int32, (rows, CHUNK), 0) == wanted
        got = dot(feat_ref[...], jnp.where(hot, 1.0, 0.0).astype(BF16))
        got = jnp.concatenate([got, jnp.zeros((FPAD - FEAT, CHUNK), F32)], axis=0).astype(BF16)
        for z in range(Z):
            height, left = spot(z, half)
            out_ref[c * Z + z] = got[height, left : left + PART]


def sum_kernel(in_ref, out_ref):
    total = in_ref[0].astype(F32)
    for i in range(1, in_ref.shape[0]):
        total = total + in_ref[i].astype(F32)
    total = total.astype(BF16)
    for i in range(out_ref.shape[0]):
        out_ref[i] = total


def split_halves(own_ref, keep_ref, send_ref):
    core = my_core()
    width = keep_ref.shape[1]
    keep_ref[...] = own_ref[:WIRE, pl.ds(pl.multiple_of(core * width, width), width)]
    send_ref[...] = own_ref[:WIRE, pl.ds(pl.multiple_of((1 - core) * width, width), width)]


def own_scores(low_ref, kern_ref, own_ref):
    @pl.loop(0, kern_ref.shape[0] // BLOCK)
    def _(n):
        at = pl.ds(pl.multiple_of(n * BLOCK, BLOCK), BLOCK)
        own_ref[:, at] = dot_nt(low_ref[...], kern_ref[at, :])


def build_kernel(
    feat_ref, norm_ref, c0, c1, c2, c3, warm_ref,
    kern_ref, coef_ref, own_ref, keep_ref, send_ref, cent_ref, low_ref,
):
    scale = LOG2E / FEAT
    half = FPAD // 2
    norms = []
    for d, c_ref in enumerate((c0, c1, c2, c3)):
        for z in range(Z):
            height, left = spot(z, half)
            left += d * CHUNK
            cent_ref[height, left : left + PART] = c_ref[z]
        cols = slice(d * CHUNK, (d + 1) * CHUNK)
        norms.append(
            jnp.sum(jnp.square(cent_ref[:, cols].astype(F32)), axis=0, keepdims=True) * scale
        )
        warm = warm_ref[:, pl.ds(pl.multiple_of(chunk_of(d) * CHUNK, CHUNK), CHUNK)]
        warm = jnp.concatenate([warm, jnp.zeros((PAD - CLASSES, CHUNK), F32)], axis=0)
        coef_ref[:, cols] = warm
        low_ref[:, cols] = warm.astype(BF16)

    @pl.loop(0, kern_ref.shape[0] // BLOCK)
    def _(n):
        at = pl.ds(pl.multiple_of(n * BLOCK, BLOCK), BLOCK)
        feats = feat_ref[at, :]
        row_norm = norm_ref[at, :] * scale
        for d in range(X):
            cols = slice(d * CHUNK, (d + 1) * CHUNK)
            cross = dot(feats, cent_ref[:, cols])
            kern_ref[at, cols] = jnp.exp2(cross * (2.0 * scale) - norms[d] - row_norm).astype(BF16)

    own_scores(low_ref, kern_ref, own_ref)
    split_halves(own_ref, keep_ref, send_ref)


def residual_of(logits, labels):
    classes = lax.broadcasted_iota(jnp.int32, logits.shape, 0)
    logits = jnp.where(classes < CLASSES, logits, -1e30)
    raised = jnp.exp(logits - jnp.max(logits, axis=0, keepdims=True))
    prob = raised / jnp.sum(raised, axis=0, keepdims=True)
    return (prob - jnp.where(classes == labels, 1.0, 0.0)).astype(BF16)


def gradient_pieces(res_ref, kern_ref, out_ref):
    half = PAD // 2

    @pl.loop(0, X)
    def _(d):
        cols = pl.ds(pl.multiple_of(d * CHUNK, CHUNK), CHUNK)
        grad = dot(res_ref[...], kern_ref[:, cols]).astype(BF16)
        for z in range(Z):
            height, left = spot(z, half)
            out_ref[chunk_of(d) * Z + z] = grad[height, left : left + PART]


def first_kernel(mine_ref, theirs_ref, own_ref, kern_ref, label_ref, out_ref, base_ref, res_ref, sum_ref):
    core = my_core()
    width = mine_ref.shape[1]
    sum_ref[:WIRE, pl.ds(pl.multiple_of(core * width, width), width)] = mine_ref[...]
    sum_ref[:WIRE, pl.ds(pl.multiple_of((1 - core) * width, width), width)] = theirs_ref[...]
    for n in range(sum_ref.shape[1] // BLOCK):
        at = slice(n * BLOCK, (n + 1) * BLOCK)
        res_ref[:, at] = residual_of(sum_ref[:, at], label_ref[:, at])
    base_ref[...] = sum_ref[...] - own_ref[...]
    gradient_pieces(res_ref, kern_ref, out_ref)


def update(coef_ref, grads, new_ref, low_ref):
    half = PAD // 2
    for d, g_ref in enumerate(grads):
        for z in range(Z):
            height, left = spot(z, half)
            cols = slice(d * CHUNK + left, d * CHUNK + left + PART)
            fresh = coef_ref[height, cols] - STEP * g_ref[z].astype(F32)
            new_ref[height, cols] = fresh
            low_ref[height, cols] = fresh.astype(BF16)


def second_kernel(coef_ref, g0, g1, g2, g3, base_ref, kern_ref, label_ref, out_ref, new_ref, res_ref, low_ref):
    update(coef_ref, (g0, g1, g2, g3), new_ref, low_ref)

    @pl.loop(0, kern_ref.shape[0] // BLOCK)
    def _(n):
        at = pl.ds(pl.multiple_of(n * BLOCK, BLOCK), BLOCK)
        logits = base_ref[:, at] + dot_nt(low_ref[...], kern_ref[at, :])
        res_ref[:, at] = residual_of(logits, label_ref[:, at])

    gradient_pieces(res_ref, kern_ref, out_ref)


def score_kernel(coef_ref, g0, g1, g2, g3, kern_ref, new_ref, own_ref, keep_ref, send_ref, low_ref):
    update(coef_ref, (g0, g1, g2, g3), new_ref, low_ref)
    own_scores(low_ref, kern_ref, own_ref)
    split_halves(own_ref, keep_ref, send_ref)


def final_kernel(coef_ref, g0, g1, g2, g3, kern_ref, coef_out_ref, keep_ref, send_ref, new_ref, low_ref, own_ref):
    update(coef_ref, (g0, g1, g2, g3), new_ref, low_ref)
    for d in range(X):
        cols = slice(d * CHUNK, (d + 1) * CHUNK)
        to = pl.ds(pl.multiple_of(chunk_of(d) * CHUNK, CHUNK), CHUNK)
        coef_out_ref[:, to] = new_ref[:CLASSES, cols]
    own_scores(low_ref, kern_ref, own_ref)
    core = my_core()
    for y in range(Y):
        for ref, k in ((keep_ref, core), (send_ref, 1 - core)):
            ref[y] = own_ref[:WIRE, pl.ds(pl.multiple_of((y * CORES + k) * LANES, LANES), LANES)]


def exchange(value, axis, groups=None):
    return lax.all_to_all(
        value, axis, split_axis=0, concat_axis=0, tiled=True, axis_index_groups=groups
    )


def sum_and_gather(pieces):
    arrived = exchange(pieces, "rows")
    copies = call(sum_kernel, like((Z, *pieces.shape[1:]), BF16), name="sum_at_owner")(arrived)
    mine = exchange(copies, "rows", Z_GROUPS)
    return [mine] + [lax.ppermute(mine, "rows", x_shift(d)) for d in range(1, X)]


def sum_over_groups(keep, send):
    half = keep + lax.ppermute(send, "centers", CORE_SWAP)
    half = exchange(jnp.broadcast_to(half, (Y, *half.shape)), "centers", Y_GROUPS).sum(axis=0)
    return half, lax.ppermute(half, "centers", CORE_SWAP)


def body(features, labels, center_index, warm_coef):
    rows = features.shape[1]
    centers = center_index.shape[1]
    labels = labels.reshape(1, rows)
    kern_type = like((rows, centers), BF16)
    coef_type = like((PAD, centers), F32)
    own_type = like((PAD, rows), F32)
    half_type = like((WIRE, rows // CORES), F32)
    last_type = like((Y, WIRE, LANES), F32)
    grad_type = like((X * Z, PAD // 2, PART), BF16)
    low = pltpu.VMEM((PAD, centers), BF16)
    res = pltpu.VMEM((PAD, rows), BF16)
    score = pltpu.VMEM((PAD, rows), F32)
    coef_scratch = pltpu.VMEM((PAD, centers), F32)

    picked = call(select_kernel, like((X * Z, FPAD // 2, PART), BF16), name="select")(
        features, center_index
    )
    row_norms = jnp.sum(jnp.square(features.astype(F32)), axis=0).reshape(rows, 1)
    feat_rows = jnp.pad(features, ((0, FPAD - FEAT), (0, 0))).T
    cents = sum_and_gather(picked)
    kern, coef, own, keep, send = call(
        build_kernel,
        [kern_type, coef_type, own_type, half_type, half_type],
        [pltpu.VMEM((FPAD, centers), BF16), low],
        name="build",
    )(feat_rows, row_norms, *cents, warm_coef)

    for round_idx in range(ROUNDS):
        mine, theirs = sum_over_groups(keep, send)
        pieces, base = call(first_kernel, [grad_type, own_type], [res, score], name="first")(
            mine, theirs, own, kern, labels
        )
        for _ in range(1, PASSES):
            grads = sum_and_gather(pieces)
            pieces, coef = call(second_kernel, [grad_type, coef_type], [res, low], name="second")(
                coef, *grads, base, kern, labels
            )
        grads = sum_and_gather(pieces)
        if round_idx < ROUNDS - 1:
            coef, own, keep, send = call(
                score_kernel, [coef_type, own_type, half_type, half_type], [low], name="scores"
            )(coef, *grads, kern)
    coef_out, keep, send = call(
        final_kernel,
        [like((CLASSES, centers), F32), last_type, last_type],
        [coef_scratch, low, score],
        name="final",
    )(coef, *grads, kern)
    part = keep + lax.ppermute(send, "centers", CORE_SWAP)
    logits_out = exchange(part, "centers", Y_GROUPS).sum(axis=0)[:CLASSES]
    return coef_out, logits_out


def solution(mesh):
    return jax.shard_map(
        body,
        mesh=mesh,
        in_specs=(P(None, "rows"), P("rows"), P("centers", None), P(None, "centers")),
        out_specs=(P(None, "centers"), P(None, ("rows", "centers"))),
        check_vma=False,
    )
```

```python
import jax
import jax.numpy as jnp
from jax import lax
from jax.experimental import pallas as pl
from jax.experimental.pallas import tpu as pltpu
from jax.sharding import PartitionSpec as P

ROUNDS = 2
PASSES = 2
STEP = 0.1

X, Z, Y, CORES = 4, 8, 4, 2
CLASSES = 147
PAD = 160
WIRE = 152
FEAT = 440
FPAD = 448
LANES = 128
CHUNK = X * LANES
PART = CHUNK // 4
BLOCK = 256
GRANT = 20 * 2**20
FLOPS = 2**30

F32 = jnp.float32
BF16 = jnp.bfloat16
LOG2E = 1.4426950408889634

X_GROUPS = [[x * Z + z for x in range(X)] for z in range(Z)]
Z_GROUPS = [[x * Z + z for z in range(Z)] for x in range(X)]
Y_GROUPS = [[y * CORES + k for y in range(Y)] for k in range(CORES)]
CORE_SWAP = [(y * CORES + k, y * CORES + 1 - k) for y in range(Y) for k in range(CORES)]


def x_shift(d):
    return [(x * Z + z, (x + d) % X * Z + z) for x in range(X) for z in range(Z)]


def y_shift(d):
    return [(y * CORES + k, (y + d) % Y * CORES + k) for y in range(Y) for k in range(CORES)]


def call(kernel, outs, scratch=(), name=None):
    vmem = pl.BlockSpec(memory_space=pltpu.VMEM)
    many = isinstance(outs, (list, tuple))
    return lambda *args: pl.pallas_call(
        kernel,
        out_shape=outs,
        in_specs=[vmem] * len(args),
        out_specs=[vmem] * len(outs) if many else vmem,
        scratch_shapes=list(scratch),
        compiler_params=pltpu.CompilerParams(vmem_limit_bytes=GRANT),
        cost_estimate=pl.CostEstimate(flops=FLOPS, bytes_accessed=2**22, transcendentals=0),
        name=name,
    )(*args)


def like(shape, dtype):
    return jax.ShapeDtypeStruct(shape, dtype)


def my_x():
    return lax.axis_index("rows") // Z


def my_core():
    return lax.rem(lax.axis_index("centers"), CORES)


def chunk_of(d):
    return lax.rem(my_x() + X - d, X)


def spot(z, rows):
    top, left = z // 4 * rows, z % 4 * PART
    return slice(top, top + rows), left


def dot(a, b):
    return jnp.dot(a, b, preferred_element_type=F32)


def dot_nt(a, b):
    return lax.dot_general(a, b, (((1,), (1,)), ((), ())), preferred_element_type=F32)


def select_kernel(feat_ref, index_ref, out_ref):
    rows = feat_ref.shape[1]
    first = lax.axis_index("rows") * rows
    half = FPAD // 2

    @pl.loop(0, X)
    def _(c):
        wanted = index_ref[:, pl.ds(pl.multiple_of(c * CHUNK, CHUNK), CHUNK)] - first
        hot = lax.broadcasted_iota(jnp.int32, (rows, CHUNK), 0) == wanted
        got = dot(feat_ref[...], jnp.where(hot, 1.0, 0.0).astype(BF16))
        got = jnp.concatenate([got, jnp.zeros((FPAD - FEAT, CHUNK), F32)], axis=0).astype(BF16)
        for z in range(Z):
            height, left = spot(z, half)
            out_ref[c * Z + z] = got[height, left : left + PART]


def sum_kernel(in_ref, out_ref):
    total = in_ref[0].astype(F32)
    for i in range(1, in_ref.shape[0]):
        total = total + in_ref[i].astype(F32)
    total = total.astype(BF16)
    for i in range(out_ref.shape[0]):
        out_ref[i] = total


def split_halves(own_ref, keep_ref, send_ref):
    core = my_core()
    width = keep_ref.shape[1]
    keep_ref[...] = own_ref[:WIRE, pl.ds(pl.multiple_of(core * width, width), width)]
    send_ref[...] = own_ref[:WIRE, pl.ds(pl.multiple_of((1 - core) * width, width), width)]


def own_scores(low_ref, kern_ref, own_ref):
    @pl.loop(0, kern_ref.shape[0] // BLOCK)
    def _(n):
        at = pl.ds(pl.multiple_of(n * BLOCK, BLOCK), BLOCK)
        own_ref[:, at] = dot_nt(low_ref[...], kern_ref[at, :])


def kernel_columns(feat_ref, norm_ref, c_ref, cent_ref, kern_ref, left):
    scale = LOG2E / FEAT
    for z in range(Z):
        height, at = spot(z, FPAD // 2)
        cent_ref[height, at : at + PART] = c_ref[z]
    center_norm = jnp.sum(jnp.square(cent_ref[...].astype(F32)), axis=0, keepdims=True) * scale

    @pl.loop(0, kern_ref.shape[0] // BLOCK)
    def _(n):
        at = pl.ds(pl.multiple_of(n * BLOCK, BLOCK), BLOCK)
        cross = dot(feat_ref[at, :], cent_ref[...])
        power = cross * (2.0 * scale) - center_norm - norm_ref[at, :] * scale
        kern_ref[at, left : left + CHUNK] = jnp.exp2(power).astype(BF16)


def chunk_kernel(feat_ref, norm_ref, c_ref, kern_ref, cent_ref):
    kernel_columns(feat_ref, norm_ref, c_ref, cent_ref, kern_ref, 0)


def build_kernel(
    feat_ref, norm_ref, c_ref, k0, k2, k3, warm_ref,
    kern_ref, coef_ref, own_ref, keep_ref, send_ref, cent_ref, low_ref,
):
    for d, k_ref in ((0, k0), (2, k2), (3, k3)):
        kern_ref[:, d * CHUNK : (d + 1) * CHUNK] = k_ref[...]
    for d in range(X):
        cols = slice(d * CHUNK, (d + 1) * CHUNK)
        warm = warm_ref[:, pl.ds(pl.multiple_of(chunk_of(d) * CHUNK, CHUNK), CHUNK)]
        warm = jnp.concatenate([warm, jnp.zeros((PAD - CLASSES, CHUNK), F32)], axis=0)
        coef_ref[:, cols] = warm
        low_ref[:, cols] = warm.astype(BF16)
    kernel_columns(feat_ref, norm_ref, c_ref, cent_ref, kern_ref, CHUNK)
    own_scores(low_ref, kern_ref, own_ref)
    split_halves(own_ref, keep_ref, send_ref)


def residual_of(logits, labels):
    classes = lax.broadcasted_iota(jnp.int32, logits.shape, 0)
    logits = jnp.where(classes < CLASSES, logits, -1e30)
    raised = jnp.exp(logits - jnp.max(logits, axis=0, keepdims=True))
    prob = raised / jnp.sum(raised, axis=0, keepdims=True)
    return (prob - jnp.where(classes == labels, 1.0, 0.0)).astype(BF16)


def gradient_pieces(res_ref, kern_ref, out_ref):
    half = PAD // 2

    @pl.loop(0, X)
    def _(d):
        cols = pl.ds(pl.multiple_of(d * CHUNK, CHUNK), CHUNK)
        grad = dot(res_ref[...], kern_ref[:, cols]).astype(BF16)
        for z in range(Z):
            height, left = spot(z, half)
            out_ref[chunk_of(d) * Z + z] = grad[height, left : left + PART]


def first_kernel(mine_ref, theirs_ref, own_ref, kern_ref, label_ref, out_ref, base_ref, res_ref, sum_ref):
    core = my_core()
    width = mine_ref.shape[1]
    sum_ref[:WIRE, pl.ds(pl.multiple_of(core * width, width), width)] = mine_ref[...]
    sum_ref[:WIRE, pl.ds(pl.multiple_of((1 - core) * width, width), width)] = theirs_ref[...]
    for n in range(sum_ref.shape[1] // BLOCK):
        at = slice(n * BLOCK, (n + 1) * BLOCK)
        res_ref[:, at] = residual_of(sum_ref[:, at], label_ref[:, at])
    base_ref[...] = sum_ref[...] - own_ref[...]
    gradient_pieces(res_ref, kern_ref, out_ref)


def update(coef_ref, grads, new_ref, low_ref):
    half = PAD // 2
    for d, g_ref in enumerate(grads):
        for z in range(Z):
            height, left = spot(z, half)
            cols = slice(d * CHUNK + left, d * CHUNK + left + PART)
            fresh = coef_ref[height, cols] - STEP * g_ref[z].astype(F32)
            new_ref[height, cols] = fresh
            low_ref[height, cols] = fresh.astype(BF16)


def second_kernel(coef_ref, g0, g1, g2, g3, base_ref, kern_ref, label_ref, out_ref, new_ref, res_ref, low_ref):
    update(coef_ref, (g0, g1, g2, g3), new_ref, low_ref)

    @pl.loop(0, kern_ref.shape[0] // BLOCK)
    def _(n):
        at = pl.ds(pl.multiple_of(n * BLOCK, BLOCK), BLOCK)
        logits = base_ref[:, at] + dot_nt(low_ref[...], kern_ref[at, :])
        res_ref[:, at] = residual_of(logits, label_ref[:, at])

    gradient_pieces(res_ref, kern_ref, out_ref)


def score_kernel(coef_ref, g0, g1, g2, g3, kern_ref, new_ref, own_ref, keep_ref, send_ref, low_ref):
    update(coef_ref, (g0, g1, g2, g3), new_ref, low_ref)
    own_scores(low_ref, kern_ref, own_ref)
    split_halves(own_ref, keep_ref, send_ref)


def final_kernel(coef_ref, g0, g1, g2, g3, kern_ref, coef_out_ref, keep_ref, send_ref, new_ref, low_ref, own_ref):
    update(coef_ref, (g0, g1, g2, g3), new_ref, low_ref)
    for d in range(X):
        cols = slice(d * CHUNK, (d + 1) * CHUNK)
        to = pl.ds(pl.multiple_of(chunk_of(d) * CHUNK, CHUNK), CHUNK)
        coef_out_ref[:, to] = new_ref[:CLASSES, cols]
    own_scores(low_ref, kern_ref, own_ref)
    core = my_core()
    for y in range(Y):
        for ref, k in ((keep_ref, core), (send_ref, 1 - core)):
            ref[y] = own_ref[:WIRE, pl.ds(pl.multiple_of((y * CORES + k) * LANES, LANES), LANES)]


def exchange(value, axis, groups=None):
    return lax.all_to_all(
        value, axis, split_axis=0, concat_axis=0, tiled=True, axis_index_groups=groups
    )


def sum_and_gather(pieces):
    arrived = exchange(pieces, "rows")
    copies = call(sum_kernel, like((Z, *pieces.shape[1:]), BF16), name="sum_at_owner")(arrived)
    mine = exchange(copies, "rows", Z_GROUPS)
    return [mine] + [lax.ppermute(mine, "rows", x_shift(d)) for d in range(1, X)]


def sum_over_groups(keep, send):
    half = keep + lax.ppermute(send, "centers", CORE_SWAP)
    others = [lax.ppermute(half, "centers", y_shift(d)) for d in (2, 1, 3)]
    half = half + others[0] + (others[1] + others[2])
    return half, lax.ppermute(half, "centers", CORE_SWAP)


def body(features, labels, center_index, warm_coef):
    rows = features.shape[1]
    centers = center_index.shape[1]
    labels = labels.reshape(1, rows)
    kern_type = like((rows, centers), BF16)
    coef_type = like((PAD, centers), F32)
    own_type = like((PAD, rows), F32)
    half_type = like((WIRE, rows // CORES), F32)
    last_type = like((Y, WIRE, LANES), F32)
    grad_type = like((X * Z, PAD // 2, PART), BF16)
    low = pltpu.VMEM((PAD, centers), BF16)
    res = pltpu.VMEM((PAD, rows), BF16)
    score = pltpu.VMEM((PAD, rows), F32)
    coef_scratch = pltpu.VMEM((PAD, centers), F32)

    picked = call(select_kernel, like((X * Z, FPAD // 2, PART), BF16), name="select")(
        features, center_index
    )
    row_norms = jnp.sum(jnp.square(features.astype(F32)), axis=0).reshape(rows, 1)
    feat_rows = jnp.pad(features, ((0, FPAD - FEAT), (0, 0))).T
    cents = sum_and_gather(picked)
    build_chunk = call(
        chunk_kernel, like((rows, CHUNK), BF16), [pltpu.VMEM((FPAD, CHUNK), BF16)], name="chunk"
    )
    chunks = [build_chunk(feat_rows, row_norms, cents[d]) for d in (0, 2, 3)]
    kern, coef, own, keep, send = call(
        build_kernel,
        [kern_type, coef_type, own_type, half_type, half_type],
        [pltpu.VMEM((FPAD, CHUNK), BF16), low],
        name="build",
    )(feat_rows, row_norms, cents[1], *chunks, warm_coef)

    for round_idx in range(ROUNDS):
        mine, theirs = sum_over_groups(keep, send)
        pieces, base = call(first_kernel, [grad_type, own_type], [res, score], name="first")(
            mine, theirs, own, kern, labels
        )
        for _ in range(1, PASSES):
            grads = sum_and_gather(pieces)
            pieces, coef = call(second_kernel, [grad_type, coef_type], [res, low], name="second")(
                coef, *grads, base, kern, labels
            )
        grads = sum_and_gather(pieces)
        if round_idx < ROUNDS - 1:
            coef, own, keep, send = call(
                score_kernel, [coef_type, own_type, half_type, half_type], [low], name="scores"
            )(coef, *grads, kern)
    coef_out, keep, send = call(
        final_kernel,
        [like((CLASSES, centers), F32), last_type, last_type],
        [coef_scratch, low, score],
        name="final",
    )(coef, *grads, kern)
    part = keep + lax.ppermute(send, "centers", CORE_SWAP)
    logits_out = exchange(part, "centers", Y_GROUPS).sum(axis=0)[:CLASSES]
    return coef_out, logits_out


def solution(mesh):
    return jax.shard_map(
        body,
        mesh=mesh,
        in_specs=(P(None, "rows"), P("rows"), P("centers", None), P(None, "centers")),
        out_specs=(P(None, "centers"), P(None, ("rows", "centers"))),
        check_vma=False,
    )
```

```python
import functools

import jax
import jax.numpy as jnp
from jax import lax
from jax.experimental import pallas as pl
from jax.experimental.pallas import tpu as pltpu
from jax.sharding import PartitionSpec as P

ROUNDS = 2
PASSES = 2
STEP = 0.1

X, Z, Y, CORES = 4, 8, 4, 2
CLASSES = 147
PAD = 160
WIRE = 152
FEAT = 440
FPAD = 448
LANES = 128
CHUNK = X * LANES
PART = CHUNK // 4
BLOCK = 256
SLOTS = 32
GRANT = 20 * 2**20
FLOPS = 2**30

F32 = jnp.float32
BF16 = jnp.bfloat16
LOG2E = 1.4426950408889634

X_GROUPS = [[x * Z + z for x in range(X)] for z in range(Z)]
Z_GROUPS = [[x * Z + z for z in range(Z)] for x in range(X)]
Y_GROUPS = [[y * CORES + k for y in range(Y)] for k in range(CORES)]
CORE_SWAP = [(y * CORES + k, y * CORES + 1 - k) for y in range(Y) for k in range(CORES)]


def x_shift(d):
    return [(x * Z + z, (x + d) % X * Z + z) for x in range(X) for z in range(Z)]


def y_shift(d):
    return [(y * CORES + k, (y + d) % Y * CORES + k) for y in range(Y) for k in range(CORES)]


def call(kernel, outs, scratch=(), name=None, scalars=0):
    vmem = pl.BlockSpec(memory_space=pltpu.VMEM)
    smem = pl.BlockSpec(memory_space=pltpu.SMEM)
    many = isinstance(outs, (list, tuple))
    return lambda *args: pl.pallas_call(
        kernel,
        out_shape=outs,
        in_specs=[smem] * scalars + [vmem] * (len(args) - scalars),
        out_specs=[vmem] * len(outs) if many else vmem,
        scratch_shapes=list(scratch),
        compiler_params=pltpu.CompilerParams(vmem_limit_bytes=GRANT),
        cost_estimate=pl.CostEstimate(flops=FLOPS, bytes_accessed=2**22, transcendentals=0),
        name=name,
    )(*args)


def like(shape, dtype):
    return jax.ShapeDtypeStruct(shape, dtype)


def my_x():
    return lax.axis_index("rows") // Z


def my_core():
    return lax.rem(lax.axis_index("centers"), CORES)


def chunk_of(d):
    return lax.rem(my_x() + X - d, X)


def spot(z, rows):
    top, left = z // 4 * rows, z % 4 * PART
    return slice(top, top + rows), left


def dot(a, b):
    return jnp.dot(a, b, preferred_element_type=F32)


def dot_nt(a, b):
    return lax.dot_general(a, b, (((1,), (1,)), ((), ())), preferred_element_type=F32)


def block_ranks(index_ref, rank_ref, rows):
    before = lax.broadcasted_iota(jnp.int32, (PART, PART), 0) < lax.broadcasted_iota(
        jnp.int32, (PART, PART), 1
    )
    before = jnp.where(before, 1.0, 0.0).astype(BF16)
    owners = lax.broadcasted_iota(jnp.int32, (X * Z, PART), 0)

    def block(b, top):
        cols = pl.ds(pl.multiple_of(b * PART, PART), PART)
        owned = jnp.where(lax.div(index_ref[:, cols], rows) == owners, 1.0, 0.0)
        rank = jnp.sum(dot(owned.astype(BF16), before) * owned, axis=0, keepdims=True)
        rank_ref[:, cols] = rank
        return jnp.maximum(top, rank)

    return lax.fori_loop(0, rank_ref.shape[1] // PART, block, jnp.zeros((1, PART), F32))


def select_kernel(turn_ref, feat_ref, index_ref, out_ref, rank_ref, top_ref, hot_ref):
    rows = feat_ref.shape[1]
    half = FPAD // 2
    top_ref[...] = jnp.broadcast_to(
        jnp.max(block_ranks(index_ref, rank_ref, rows), axis=1, keepdims=True), top_ref.shape
    )
    first = lax.axis_index("rows") * rows
    skip = (turn_ref[0] * SLOTS).astype(F32)
    slots = lax.broadcasted_iota(jnp.int32, (SLOTS, PART), 0).astype(F32)
    places = lax.broadcasted_iota(jnp.int32, (SLOTS, rows), 1).astype(F32)

    @pl.loop(0, rank_ref.shape[1] // PART)
    def _(b):
        cols = pl.ds(pl.multiple_of(b * PART, PART), PART)
        local = index_ref[:, cols] - first
        inside = (local >= 0) & (local < rows)
        chosen = inside & (rank_ref[:, cols] - skip == slots)
        place = jnp.sum(
            jnp.where(chosen, (local + 1).astype(F32), 0.0), axis=1, keepdims=True
        )
        hot_ref[pl.ds(pl.multiple_of(b * SLOTS, SLOTS), SLOTS), :] = jnp.where(places == place - 1.0, 1.0, 0.0).astype(BF16)
    out_ref[...] = jnp.zeros_like(out_ref)
    for h, stop in ((0, half), (1, FEAT)):
        got = dot_nt(hot_ref[...], feat_ref[h * half : stop, :]).astype(BF16)
        for b in range(rank_ref.shape[1] // PART):
            to = b // 4 * Z + h * 4 + b % 4
            out_ref[to, :, : stop - h * half] = got[b * SLOTS : (b + 1) * SLOTS]


def place_kernel(turn_ref, in_ref, index_ref, rank_ref, out_ref, *, rows):
    me = lax.axis_index("rows")
    block = lax.div(me, Z) * 4 + lax.rem(me, 4)
    cols = pl.ds(pl.multiple_of(block * PART, PART), PART)
    rank = rank_ref[:, cols].astype(jnp.int32) - turn_ref[0] * SLOTS
    slot = lax.div(index_ref[:, cols], rows) * SLOTS + rank
    slot = jnp.where((rank >= 0) & (rank < SLOTS), slot, -1)
    count = in_ref.shape[0] * SLOTS
    hot = lax.broadcasted_iota(jnp.int32, (count, PART), 0) == slot
    hot = jnp.where(hot, 1.0, 0.0).astype(BF16)
    arrived = in_ref[...].reshape(count, in_ref.shape[2])
    placed = lax.dot_general(
        arrived, hot, (((0,), (0,)), ((), ())), preferred_element_type=F32
    ).astype(BF16)
    for i in range(out_ref.shape[0]):
        out_ref[i] = placed[: FPAD // 2]


def sum_kernel(in_ref, out_ref):
    total = lax.fori_loop(
        0, in_ref.shape[0] // 4,
        lambda i, total: total + sum(in_ref[i * 4 + j].astype(F32) for j in range(4)),
        jnp.zeros(in_ref.shape[1:], F32),
    ).astype(BF16)
    for i in range(out_ref.shape[0]):
        out_ref[i] = total


def split_halves(own_ref, keep_ref, send_ref):
    core = my_core()
    width = keep_ref.shape[1]
    keep_ref[...] = own_ref[:WIRE, pl.ds(pl.multiple_of(core * width, width), width)]
    send_ref[...] = own_ref[:WIRE, pl.ds(pl.multiple_of((1 - core) * width, width), width)]


def own_scores(low_ref, kern_ref, own_ref):
    @pl.loop(0, kern_ref.shape[0] // BLOCK)
    def _(n):
        at = pl.ds(pl.multiple_of(n * BLOCK, BLOCK), BLOCK)
        own_ref[:, at] = dot_nt(low_ref[...], kern_ref[at, :])


def kernel_columns(feat_ref, norm_ref, c_ref, cent_ref, kern_ref, left):
    scale = LOG2E / FEAT
    for z in range(Z):
        height, at = spot(z, FPAD // 2)
        cent_ref[height, at : at + PART] = c_ref[z]
    center_norm = jnp.sum(jnp.square(cent_ref[...].astype(F32)), axis=0, keepdims=True) * scale

    @pl.loop(0, kern_ref.shape[0] // BLOCK)
    def _(n):
        at = pl.ds(pl.multiple_of(n * BLOCK, BLOCK), BLOCK)
        cross = dot(feat_ref[at, :], cent_ref[...])
        power = cross * (2.0 * scale) - center_norm - norm_ref[at, :] * scale
        kern_ref[at, left : left + CHUNK] = jnp.exp2(power).astype(BF16)


def chunk_kernel(feat_ref, norm_ref, c_ref, kern_ref, cent_ref):
    kernel_columns(feat_ref, norm_ref, c_ref, cent_ref, kern_ref, 0)


def build_kernel(
    feat_ref, norm_ref, c_ref, k0, k2, k3, warm_ref,
    kern_ref, coef_ref, own_ref, keep_ref, send_ref, cent_ref, low_ref,
):
    for d, k_ref in ((0, k0), (2, k2), (3, k3)):
        kern_ref[:, d * CHUNK : (d + 1) * CHUNK] = k_ref[...]
    for d in range(X):
        cols = slice(d * CHUNK, (d + 1) * CHUNK)
        warm = warm_ref[:, pl.ds(pl.multiple_of(chunk_of(d) * CHUNK, CHUNK), CHUNK)]
        warm = jnp.concatenate([warm, jnp.zeros((PAD - CLASSES, CHUNK), F32)], axis=0)
        coef_ref[:, cols] = warm
        low_ref[:, cols] = warm.astype(BF16)
    kernel_columns(feat_ref, norm_ref, c_ref, cent_ref, kern_ref, CHUNK)
    own_scores(low_ref, kern_ref, own_ref)
    split_halves(own_ref, keep_ref, send_ref)


def residual_of(logits, labels):
    classes = lax.broadcasted_iota(jnp.int32, logits.shape, 0)
    logits = jnp.where(classes < CLASSES, logits, -1e30)
    raised = jnp.exp(logits - jnp.max(logits, axis=0, keepdims=True))
    prob = raised / jnp.sum(raised, axis=0, keepdims=True)
    return (prob - jnp.where(classes == labels, 1.0, 0.0)).astype(BF16)


def gradient_pieces(res_ref, kern_ref, out_ref):
    half = PAD // 2

    @pl.loop(0, X)
    def _(d):
        cols = pl.ds(pl.multiple_of(d * CHUNK, CHUNK), CHUNK)
        grad = dot(res_ref[...], kern_ref[:, cols]).astype(BF16)
        for z in range(Z):
            height, left = spot(z, half)
            out_ref[chunk_of(d) * Z + z] = grad[height, left : left + PART]


def first_kernel(m0, m1, t0, t1, own_ref, kern_ref, label_ref, out_ref, base_ref, res_ref, sum_ref):
    core = my_core()
    width = m0.shape[1]
    for side, refs in ((core, (m0, m1)), (1 - core, (t0, t1))):
        for i, ref in enumerate(refs):
            to = pl.multiple_of((side * 2 + i) * width, width)
            sum_ref[:WIRE, pl.ds(to, width)] = ref[...]
    for n in range(sum_ref.shape[1] // BLOCK):
        at = slice(n * BLOCK, (n + 1) * BLOCK)
        res_ref[:, at] = residual_of(sum_ref[:, at], label_ref[:, at])
    base_ref[...] = sum_ref[...] - own_ref[...]
    gradient_pieces(res_ref, kern_ref, out_ref)


def update(coef_ref, grads, new_ref, low_ref):
    half = PAD // 2

    @pl.loop(0, Z)
    def _(z):
        height = pl.ds(pl.multiple_of(lax.div(z, 4) * half, half), half)
        for d, g_ref in enumerate(grads):
            left = pl.multiple_of(d * CHUNK + lax.rem(z, 4) * PART, PART)
            cols = pl.ds(left, PART)
            fresh = coef_ref[height, cols] - STEP * g_ref[z].astype(F32)
            new_ref[height, cols] = fresh
            low_ref[height, cols] = fresh.astype(BF16)


def second_kernel(coef_ref, g0, g1, g2, g3, base_ref, kern_ref, label_ref, out_ref, new_ref, res_ref, low_ref):
    update(coef_ref, (g0, g1, g2, g3), new_ref, low_ref)

    @pl.loop(0, kern_ref.shape[0] // BLOCK)
    def _(n):
        at = pl.ds(pl.multiple_of(n * BLOCK, BLOCK), BLOCK)
        logits = base_ref[:, at] + dot_nt(low_ref[...], kern_ref[at, :])
        res_ref[:, at] = residual_of(logits, label_ref[:, at])

    gradient_pieces(res_ref, kern_ref, out_ref)


def score_kernel(coef_ref, g0, g1, g2, g3, kern_ref, new_ref, own_ref, keep_ref, send_ref, low_ref):
    update(coef_ref, (g0, g1, g2, g3), new_ref, low_ref)
    own_scores(low_ref, kern_ref, own_ref)
    split_halves(own_ref, keep_ref, send_ref)


def final_kernel(coef_ref, g0, g1, g2, g3, kern_ref, coef_out_ref, keep_ref, send_ref, new_ref, low_ref, own_ref):
    update(coef_ref, (g0, g1, g2, g3), new_ref, low_ref)
    for d in range(X):
        cols = slice(d * CHUNK, (d + 1) * CHUNK)
        to = pl.ds(pl.multiple_of(chunk_of(d) * CHUNK, CHUNK), CHUNK)
        coef_out_ref[:, to] = new_ref[:CLASSES, cols]
    own_scores(low_ref, kern_ref, own_ref)
    core = my_core()
    for y in range(Y):
        for ref, k in ((keep_ref, core), (send_ref, 1 - core)):
            ref[y] = own_ref[:WIRE, pl.ds(pl.multiple_of((y * CORES + k) * LANES, LANES), LANES)]


def exchange(value, axis, groups=None):
    return lax.all_to_all(
        value, axis, split_axis=0, concat_axis=0, tiled=True, axis_index_groups=groups
    )


def gather(copies):
    mine = exchange(copies, "rows", Z_GROUPS)
    return [mine] + [lax.ppermute(mine, "rows", x_shift(d)) for d in range(1, X)]


def sum_and_gather(pieces):
    arrived = exchange(pieces, "rows")
    copies = call(sum_kernel, like((Z, *pieces.shape[1:]), BF16), name="sum_at_owner")(arrived)
    return gather(copies)


def gather_centers(features, center_index):
    rows = features.shape[1]
    centers = center_index.shape[1]

    def select(turn):
        return call(
            select_kernel,
            [
                like((X * Z, SLOTS, 256), BF16),
                like((1, centers), F32),
                like((8, LANES), F32),
            ],
            [pltpu.VMEM((centers // PART * SLOTS, rows), BF16)],
            name="select",
            scalars=1,
        )(turn, features, center_index)

    def place(turn, pieces, rank):
        arrived = exchange(pieces, "rows")
        return call(
            functools.partial(place_kernel, rows=rows),
            like((Z, FPAD // 2, PART), BF16),
            name="place",
            scalars=1,
        )(turn, arrived, center_index, rank)

    start = jnp.zeros((1,), jnp.int32)
    pieces, rank, top = select(start)
    top = jnp.maximum(top, lax.ppermute(top, "centers", CORE_SWAP))
    pieces, top = lax.optimization_barrier((pieces, top))
    tops = [lax.ppermute(top, "centers", y_shift(d)) for d in (2, 1, 3)]
    copies = place(start, pieces, rank)
    for other in tops:
        top = jnp.maximum(top, other)
    last = top[0, 0].astype(jnp.int32)

    def another(state):
        turn, copies = state
        pieces, rank, _ = select(turn)
        return turn + 1, copies + place(turn, pieces, rank)

    _, copies = lax.while_loop(
        lambda state: state[0][0] * SLOTS <= last, another, (start + 1, copies)
    )
    return gather(copies)


def pairwise(axis_map):
    return [(y * CORES + k, axis_map(y) * CORES + k) for y in range(Y) for k in range(CORES)]


def sum_over_groups(keep, send):
    half = keep + lax.ppermute(send, "centers", CORE_SWAP)
    width = half.shape[1] // 2
    steps = (pairwise(lambda y: y ^ 1), pairwise(lambda y: Y - 1 - y))
    parts = [half[:, :width], half[:, width:]]
    for order in (steps, steps[::-1]):
        parts = [p + lax.ppermute(p, "centers", step) for p, step in zip(parts, order)]
    return parts + [lax.ppermute(p, "centers", CORE_SWAP) for p in parts]


def body(features, labels, center_index, warm_coef):
    rows = features.shape[1]
    centers = center_index.shape[1]
    labels = labels.reshape(1, rows)
    kern_type = like((rows, centers), BF16)
    coef_type = like((PAD, centers), F32)
    own_type = like((PAD, rows), F32)
    half_type = like((WIRE, rows // CORES), F32)
    last_type = like((Y, WIRE, LANES), F32)
    grad_type = like((X * Z, PAD // 2, PART), BF16)
    low = pltpu.VMEM((PAD, centers), BF16)
    res = pltpu.VMEM((PAD, rows), BF16)
    score = pltpu.VMEM((PAD, rows), F32)
    coef_scratch = pltpu.VMEM((PAD, centers), F32)

    row_norms = jnp.sum(jnp.square(features.astype(F32)), axis=0).reshape(rows, 1)
    feat_rows = jnp.pad(features, ((0, FPAD - FEAT), (0, 0))).T
    cents = gather_centers(features, center_index)
    build_chunk = call(
        chunk_kernel, like((rows, CHUNK), BF16), [pltpu.VMEM((FPAD, CHUNK), BF16)], name="chunk"
    )
    chunks = [build_chunk(feat_rows, row_norms, cents[d]) for d in (0, 2, 3)]
    kern, coef, own, keep, send = call(
        build_kernel,
        [kern_type, coef_type, own_type, half_type, half_type],
        [pltpu.VMEM((FPAD, CHUNK), BF16), low],
        name="build",
    )(feat_rows, row_norms, cents[1], *chunks, warm_coef)

    for round_idx in range(ROUNDS):
        sums = sum_over_groups(keep, send)
        pieces, base = call(first_kernel, [grad_type, own_type], [res, score], name="first")(
            *sums, own, kern, labels
        )
        for _ in range(1, PASSES):
            grads = sum_and_gather(pieces)
            pieces, coef = call(second_kernel, [grad_type, coef_type], [res, low], name="second")(
                coef, *grads, base, kern, labels
            )
        grads = sum_and_gather(pieces)
        if round_idx < ROUNDS - 1:
            coef, own, keep, send = call(
                score_kernel, [coef_type, own_type, half_type, half_type], [low], name="scores"
            )(coef, *grads, kern)
    coef_out, keep, send = call(
        final_kernel,
        [like((CLASSES, centers), F32), last_type, last_type],
        [coef_scratch, low, score],
        name="final",
    )(coef, *grads, kern)
    part = keep + lax.ppermute(send, "centers", CORE_SWAP)
    logits_out = exchange(part, "centers", Y_GROUPS).sum(axis=0)[:CLASSES]
    return coef_out, logits_out


def solution(mesh):
    return jax.shard_map(
        body,
        mesh=mesh,
        in_specs=(P(None, "rows"), P("rows"), P("centers", None), P(None, "centers")),
        out_specs=(P(None, "centers"), P(None, ("rows", "centers"))),
        check_vma=False,
    )
```

```python
import functools

import jax
import jax.numpy as jnp
from jax import lax
from jax.experimental import pallas as pl
from jax.experimental.pallas import tpu as pltpu
from jax.sharding import PartitionSpec as P

ROUNDS = 2
PASSES = 2
STEP = 0.1

X, Z, Y, CORES = 4, 8, 4, 2
CLASSES = 147
PAD = 160
WIRE = 152
FEAT = 440
FPAD = 448
LANES = 128
CHUNK = X * LANES
PART = CHUNK // 4
BLOCK = 256
SLOTS = 32
GRANT = 20 * 2**20
FLOPS = 2**30

F32 = jnp.float32
BF16 = jnp.bfloat16
LOG2E = 1.4426950408889634

X_GROUPS = [[x * Z + z for x in range(X)] for z in range(Z)]
Z_GROUPS = [[x * Z + z for z in range(Z)] for x in range(X)]
Y_GROUPS = [[y * CORES + k for y in range(Y)] for k in range(CORES)]
CORE_SWAP = [(y * CORES + k, y * CORES + 1 - k) for y in range(Y) for k in range(CORES)]


def x_shift(d):
    return [(x * Z + z, (x + d) % X * Z + z) for x in range(X) for z in range(Z)]


def y_shift(d):
    return [(y * CORES + k, (y + d) % Y * CORES + k) for y in range(Y) for k in range(CORES)]


def call(kernel, outs, scratch=(), name=None, scalars=0, last_scalar=False):
    vmem = pl.BlockSpec(memory_space=pltpu.VMEM)
    smem = pl.BlockSpec(memory_space=pltpu.SMEM)
    many = isinstance(outs, (list, tuple))
    return lambda *args: pl.pallas_call(
        kernel,
        out_shape=outs,
        in_specs=[smem] * scalars + [vmem] * (len(args) - scalars),
        out_specs=([vmem] * (len(outs) - last_scalar) + [smem] * last_scalar) if many else vmem,
        scratch_shapes=list(scratch),
        compiler_params=pltpu.CompilerParams(vmem_limit_bytes=GRANT),
        cost_estimate=pl.CostEstimate(flops=FLOPS, bytes_accessed=2**22, transcendentals=0),
        name=name,
    )(*args)


def like(shape, dtype):
    return jax.ShapeDtypeStruct(shape, dtype)


def my_x():
    return lax.axis_index("rows") // Z


def my_core():
    return lax.rem(lax.axis_index("centers"), CORES)


def chunk_of(d):
    return lax.rem(my_x() + X - d, X)


def spot(z, rows):
    top, left = z // 4 * rows, z % 4 * PART
    return slice(top, top + rows), left


def dot(a, b):
    return jnp.dot(a, b, preferred_element_type=F32)


def dot_nt(a, b):
    return lax.dot_general(a, b, (((1,), (1,)), ((), ())), preferred_element_type=F32)


def block_ranks(owner):
    before = lax.broadcasted_iota(jnp.int32, (PART, PART), 0) < lax.broadcasted_iota(
        jnp.int32, (PART, PART), 1
    )
    before = jnp.where(before, 1.0, 0.0).astype(BF16)
    owned = [jnp.where(owner == device, 1.0, 0.0) for device in range(X * Z)]
    earlier = dot(jnp.concatenate(owned, axis=0).astype(BF16), before)
    blocks = owner.shape[0]
    return sum(
        one * earlier[device * blocks : (device + 1) * blocks] for device, one in enumerate(owned)
    )


def select_kernel(turn_ref, feat_ref, index_ref, out_ref, rank_ref, top_ref, hot_ref):
    rows = feat_ref.shape[1]
    blocks = index_ref.shape[0]
    half = FPAD // 2
    rank = block_ranks(lax.div(index_ref[...], rows))
    rank_ref[...] = rank
    top_ref[0] = jnp.max(rank).astype(jnp.int32)
    first = lax.axis_index("rows") * rows
    skip = (turn_ref[0] * SLOTS).astype(F32)
    slots = lax.broadcasted_iota(jnp.int32, (SLOTS, PART), 0).astype(F32)
    places = lax.broadcasted_iota(jnp.int32, (SLOTS, rows), 1).astype(F32)
    out_ref[...] = jnp.zeros_like(out_ref)

    def find(b, _):
        local = index_ref[pl.ds(b, 1), :] - first
        inside = (local >= 0) & (local < rows)
        chosen = inside & (rank_ref[pl.ds(b, 1), :] - skip == slots)
        place = jnp.sum(jnp.where(chosen, (local + 1).astype(F32), 0.0), axis=1, keepdims=True)
        hot = jnp.where(places == place - 1.0, 1.0, 0.0).astype(BF16)
        hot_ref[pl.ds(pl.multiple_of(b * SLOTS, SLOTS), SLOTS), :] = hot
        return 0

    lax.fori_loop(0, blocks, find, 0, unroll=4)
    for h, stop in ((0, half), (1, FEAT)):
        got = dot_nt(hot_ref[...], feat_ref[h * half : stop, :]).astype(BF16)
        for b in range(blocks):
            to = b // 4 * Z + h * 4 + b % 4
            out_ref[to, :, : stop - h * half] = got[b * SLOTS : (b + 1) * SLOTS]


def place_kernel(turn_ref, in_ref, index_ref, rank_ref, out_ref, *, rows):
    me = lax.axis_index("rows")
    block = pl.ds(lax.div(me, Z) * 4 + lax.rem(me, 4), 1)
    rank = rank_ref[block, :].astype(jnp.int32) - turn_ref[0] * SLOTS
    slot = lax.div(index_ref[block, :], rows) * SLOTS + rank
    slot = jnp.where((rank >= 0) & (rank < SLOTS), slot, -1)
    count = in_ref.shape[0] * SLOTS
    hot = lax.broadcasted_iota(jnp.int32, (count, PART), 0) == slot
    hot = jnp.where(hot, 1.0, 0.0).astype(BF16)
    arrived = in_ref[...].reshape(count, in_ref.shape[2])
    placed = lax.dot_general(
        arrived, hot, (((0,), (0,)), ((), ())), preferred_element_type=F32
    ).astype(BF16)
    for i in range(out_ref.shape[0]):
        out_ref[i] = placed[: FPAD // 2]


def sum_kernel(in_ref, out_ref):
    total = lax.fori_loop(
        0, in_ref.shape[0] // 4,
        lambda i, total: total + sum(in_ref[i * 4 + j].astype(F32) for j in range(4)),
        jnp.zeros(in_ref.shape[1:], F32),
    ).astype(BF16)
    for i in range(out_ref.shape[0]):
        out_ref[i] = total


def split_halves(own_ref, keep_ref, send_ref):
    core = my_core()
    width = keep_ref.shape[1]
    keep_ref[...] = own_ref[:WIRE, pl.ds(pl.multiple_of(core * width, width), width)]
    send_ref[...] = own_ref[:WIRE, pl.ds(pl.multiple_of((1 - core) * width, width), width)]


def own_scores(low_ref, kern_ref, own_ref):
    @pl.loop(0, kern_ref.shape[0] // BLOCK)
    def _(n):
        at = pl.ds(pl.multiple_of(n * BLOCK, BLOCK), BLOCK)
        own_ref[:, at] = dot_nt(low_ref[...], kern_ref[at, :])


def kernel_columns(feat_ref, norm_ref, c_ref, cent_ref, kern_ref, left):
    scale = LOG2E / FEAT
    for z in range(Z):
        height, at = spot(z, FPAD // 2)
        cent_ref[height, at : at + PART] = c_ref[z]
    center_norm = jnp.sum(jnp.square(cent_ref[...].astype(F32)), axis=0, keepdims=True) * scale

    @pl.loop(0, kern_ref.shape[0] // BLOCK)
    def _(n):
        at = pl.ds(pl.multiple_of(n * BLOCK, BLOCK), BLOCK)
        cross = dot(feat_ref[at, :], cent_ref[...])
        power = cross * (2.0 * scale) - center_norm - norm_ref[at, :] * scale
        kern_ref[at, left : left + CHUNK] = jnp.exp2(power).astype(BF16)


def chunk_kernel(feat_ref, norm_ref, c_ref, kern_ref, cent_ref):
    kernel_columns(feat_ref, norm_ref, c_ref, cent_ref, kern_ref, 0)


def build_kernel(
    feat_ref, norm_ref, c_ref, k0, k2, k3, warm_ref,
    kern_ref, coef_ref, own_ref, keep_ref, send_ref, cent_ref, low_ref,
):
    for d, k_ref in ((0, k0), (2, k2), (3, k3)):
        kern_ref[:, d * CHUNK : (d + 1) * CHUNK] = k_ref[...]
    for d in range(X):
        cols = slice(d * CHUNK, (d + 1) * CHUNK)
        warm = warm_ref[:, pl.ds(pl.multiple_of(chunk_of(d) * CHUNK, CHUNK), CHUNK)]
        warm = jnp.concatenate([warm, jnp.zeros((PAD - CLASSES, CHUNK), F32)], axis=0)
        coef_ref[:, cols] = warm
        low_ref[:, cols] = warm.astype(BF16)
    kernel_columns(feat_ref, norm_ref, c_ref, cent_ref, kern_ref, CHUNK)
    own_scores(low_ref, kern_ref, own_ref)
    split_halves(own_ref, keep_ref, send_ref)


def residual_of(logits, labels):
    classes = lax.broadcasted_iota(jnp.int32, logits.shape, 0)
    logits = jnp.where(classes < CLASSES, logits, -1e30)
    raised = jnp.exp(logits - jnp.max(logits, axis=0, keepdims=True))
    prob = raised / jnp.sum(raised, axis=0, keepdims=True)
    return (prob - jnp.where(classes == labels, 1.0, 0.0)).astype(BF16)


def gradient_pieces(res_ref, kern_ref, out_ref):
    half = PAD // 2

    @pl.loop(0, X)
    def _(d):
        cols = pl.ds(pl.multiple_of(d * CHUNK, CHUNK), CHUNK)
        grad = dot(res_ref[...], kern_ref[:, cols]).astype(BF16)
        for z in range(Z):
            height, left = spot(z, half)
            out_ref[chunk_of(d) * Z + z] = grad[height, left : left + PART]


def first_kernel(m0, m1, t0, t1, own_ref, kern_ref, label_ref, out_ref, base_ref, res_ref, sum_ref):
    core = my_core()
    width = m0.shape[1]
    for side, refs in ((core, (m0, m1)), (1 - core, (t0, t1))):
        for i, ref in enumerate(refs):
            to = pl.multiple_of((side * 2 + i) * width, width)
            sum_ref[:WIRE, pl.ds(to, width)] = ref[...]
    for n in range(sum_ref.shape[1] // BLOCK):
        at = slice(n * BLOCK, (n + 1) * BLOCK)
        res_ref[:, at] = residual_of(sum_ref[:, at], label_ref[:, at])
    base_ref[...] = sum_ref[...] - own_ref[...]
    gradient_pieces(res_ref, kern_ref, out_ref)


def update(coef_ref, grads, new_ref, low_ref):
    half = PAD // 2

    @pl.loop(0, Z)
    def _(z):
        height = pl.ds(pl.multiple_of(lax.div(z, 4) * half, half), half)
        for d, g_ref in enumerate(grads):
            left = pl.multiple_of(d * CHUNK + lax.rem(z, 4) * PART, PART)
            cols = pl.ds(left, PART)
            fresh = coef_ref[height, cols] - STEP * g_ref[z].astype(F32)
            new_ref[height, cols] = fresh
            low_ref[height, cols] = fresh.astype(BF16)


def second_kernel(coef_ref, g0, g1, g2, g3, base_ref, kern_ref, label_ref, out_ref, new_ref, res_ref, low_ref):
    update(coef_ref, (g0, g1, g2, g3), new_ref, low_ref)

    @pl.loop(0, kern_ref.shape[0] // BLOCK)
    def _(n):
        at = pl.ds(pl.multiple_of(n * BLOCK, BLOCK), BLOCK)
        logits = base_ref[:, at] + dot_nt(low_ref[...], kern_ref[at, :])
        res_ref[:, at] = residual_of(logits, label_ref[:, at])

    gradient_pieces(res_ref, kern_ref, out_ref)


def score_kernel(coef_ref, g0, g1, g2, g3, kern_ref, new_ref, own_ref, keep_ref, send_ref, low_ref):
    update(coef_ref, (g0, g1, g2, g3), new_ref, low_ref)
    own_scores(low_ref, kern_ref, own_ref)
    split_halves(own_ref, keep_ref, send_ref)


def final_kernel(coef_ref, g0, g1, g2, g3, kern_ref, coef_out_ref, keep_ref, send_ref, new_ref, low_ref, own_ref):
    update(coef_ref, (g0, g1, g2, g3), new_ref, low_ref)
    for d in range(X):
        cols = slice(d * CHUNK, (d + 1) * CHUNK)
        to = pl.ds(pl.multiple_of(chunk_of(d) * CHUNK, CHUNK), CHUNK)
        coef_out_ref[:, to] = new_ref[:CLASSES, cols]
    own_scores(low_ref, kern_ref, own_ref)
    core = my_core()
    for y in range(Y):
        for ref, k in ((keep_ref, core), (send_ref, 1 - core)):
            ref[y] = own_ref[:WIRE, pl.ds(pl.multiple_of((y * CORES + k) * LANES, LANES), LANES)]


def exchange(value, axis, groups=None):
    return lax.all_to_all(
        value, axis, split_axis=0, concat_axis=0, tiled=True, axis_index_groups=groups
    )


def gather(copies):
    mine = exchange(copies, "rows", Z_GROUPS)
    return [mine] + [lax.ppermute(mine, "rows", x_shift(d)) for d in range(1, X)]


def sum_and_gather(pieces):
    arrived = exchange(pieces, "rows")
    copies = call(sum_kernel, like((Z, *pieces.shape[1:]), BF16), name="sum_at_owner")(arrived)
    return gather(copies)


def gather_centers(features, center_index):
    rows = features.shape[1]
    index = center_index.reshape(-1, PART)

    def select(turn):
        return call(
            select_kernel,
            [like((X * Z, SLOTS, 256), BF16), like(index.shape, F32), like((1,), jnp.int32)],
            [pltpu.VMEM((index.shape[0] * SLOTS, rows), BF16)],
            name="select",
            scalars=1,
            last_scalar=True,
        )(turn, features, index)

    def place(turn, pieces, rank):
        return call(
            functools.partial(place_kernel, rows=rows),
            like((Z, FPAD // 2, PART), BF16),
            name="place",
            scalars=1,
        )(turn, exchange(pieces, "rows"), index, rank)

    start = jnp.zeros((1,), jnp.int32)
    pieces, rank, top = select(start)
    copies = place(start, pieces, rank)

    def another(state):
        turn, copies = state
        pieces, rank, _ = select(turn)
        return turn + 1, copies + place(turn, pieces, rank)

    _, copies = lax.while_loop(
        lambda state: state[0][0] * SLOTS <= top[0], another, (start + 1, copies)
    )
    return gather(copies)


def pairwise(axis_map):
    return [(y * CORES + k, axis_map(y) * CORES + k) for y in range(Y) for k in range(CORES)]


def sum_over_groups(keep, send):
    half = keep + lax.ppermute(send, "centers", CORE_SWAP)
    width = half.shape[1] // 2
    steps = (pairwise(lambda y: y ^ 1), pairwise(lambda y: Y - 1 - y))
    parts = [half[:, :width], half[:, width:]]
    for order in (steps, steps[::-1]):
        parts = [p + lax.ppermute(p, "centers", step) for p, step in zip(parts, order)]
    return parts + [lax.ppermute(p, "centers", CORE_SWAP) for p in parts]


def body(features, labels, center_index, warm_coef):
    rows = features.shape[1]
    centers = center_index.shape[1]
    labels = labels.reshape(1, rows)
    kern_type = like((rows, centers), BF16)
    coef_type = like((PAD, centers), F32)
    own_type = like((PAD, rows), F32)
    half_type = like((WIRE, rows // CORES), F32)
    last_type = like((Y, WIRE, LANES), F32)
    grad_type = like((X * Z, PAD // 2, PART), BF16)
    low = pltpu.VMEM((PAD, centers), BF16)
    res = pltpu.VMEM((PAD, rows), BF16)
    score = pltpu.VMEM((PAD, rows), F32)
    coef_scratch = pltpu.VMEM((PAD, centers), F32)

    row_norms = jnp.sum(jnp.square(features.astype(F32)), axis=0).reshape(rows, 1)
    feat_rows = jnp.pad(features, ((0, FPAD - FEAT), (0, 0))).T
    cents = gather_centers(features, center_index)
    build_chunk = call(
        chunk_kernel, like((rows, CHUNK), BF16), [pltpu.VMEM((FPAD, CHUNK), BF16)], name="chunk"
    )
    chunks = [build_chunk(feat_rows, row_norms, cents[d]) for d in (0, 2, 3)]
    kern, coef, own, keep, send = call(
        build_kernel,
        [kern_type, coef_type, own_type, half_type, half_type],
        [pltpu.VMEM((FPAD, CHUNK), BF16), low],
        name="build",
    )(feat_rows, row_norms, cents[1], *chunks, warm_coef)

    for round_idx in range(ROUNDS):
        sums = sum_over_groups(keep, send)
        pieces, base = call(first_kernel, [grad_type, own_type], [res, score], name="first")(
            *sums, own, kern, labels
        )
        for _ in range(1, PASSES):
            grads = sum_and_gather(pieces)
            pieces, coef = call(second_kernel, [grad_type, coef_type], [res, low], name="second")(
                coef, *grads, base, kern, labels
            )
        grads = sum_and_gather(pieces)
        if round_idx < ROUNDS - 1:
            coef, own, keep, send = call(
                score_kernel, [coef_type, own_type, half_type, half_type], [low], name="scores"
            )(coef, *grads, kern)
    coef_out, keep, send = call(
        final_kernel,
        [like((CLASSES, centers), F32), last_type, last_type],
        [coef_scratch, low, score],
        name="final",
    )(coef, *grads, kern)
    part = keep + lax.ppermute(send, "centers", CORE_SWAP)
    logits_out = exchange(part, "centers", Y_GROUPS).sum(axis=0)[:CLASSES]
    return coef_out, logits_out


def solution(mesh):
    return jax.shard_map(
        body,
        mesh=mesh,
        in_specs=(P(None, "rows"), P("rows"), P("centers", None), P(None, "centers")),
        out_specs=(P(None, "centers"), P(None, ("rows", "centers"))),
        check_vma=False,
    )
```

```python
import functools

import jax
import jax.numpy as jnp
from jax import lax
from jax.experimental import pallas as pl
from jax.experimental.pallas import tpu as pltpu
from jax.sharding import PartitionSpec as P

ROUNDS = 2
PASSES = 2
STEP = 0.1

X, Z, Y, CORES = 4, 8, 4, 2
CLASSES = 147
PAD = 160
WIRE = 152
FEAT = 440
FPAD = 448
LANES = 128
CHUNK = X * LANES
PART = CHUNK // 4
BLOCK = 256
SLOTS = 16
GRANT = 20 * 2**20
FLOPS = 2**30

F32 = jnp.float32
BF16 = jnp.bfloat16
LOG2E = 1.4426950408889634

Z_GROUPS = [[x * Z + z for z in range(Z)] for x in range(X)]
CORE_SWAP = [(y * CORES + k, y * CORES + 1 - k) for y in range(Y) for k in range(CORES)]


def x_shift(d):
    return [(x * Z + z, (x + d) % X * Z + z) for x in range(X) for z in range(Z)]


def y_shift(d):
    return [(y * CORES + k, (y + d) % Y * CORES + k) for y in range(Y) for k in range(CORES)]


def call(kernel, outs, scratch=(), name=None, scalars=0, last_scalar=False):
    vmem = pl.BlockSpec(memory_space=pltpu.VMEM)
    smem = pl.BlockSpec(memory_space=pltpu.SMEM)
    many = isinstance(outs, (list, tuple))
    return lambda *args: pl.pallas_call(
        kernel,
        out_shape=outs,
        in_specs=[smem] * scalars + [vmem] * (len(args) - scalars),
        out_specs=([vmem] * (len(outs) - last_scalar) + [smem] * last_scalar) if many else vmem,
        scratch_shapes=list(scratch),
        compiler_params=pltpu.CompilerParams(vmem_limit_bytes=GRANT),
        cost_estimate=pl.CostEstimate(flops=FLOPS, bytes_accessed=2**22, transcendentals=0),
        name=name,
    )(*args)


def like(shape, dtype):
    return jax.ShapeDtypeStruct(shape, dtype)


def my_x():
    return lax.axis_index("rows") // Z


def my_core():
    return lax.rem(lax.axis_index("centers"), CORES)


def chunk_of(d):
    return lax.rem(my_x() + X - d, X)


def spot(z, rows):
    top, left = z // 4 * rows, z % 4 * PART
    return slice(top, top + rows), left


def dot(a, b):
    return jnp.dot(a, b, preferred_element_type=F32)


def dot_nt(a, b):
    return lax.dot_general(a, b, (((1,), (1,)), ((), ())), preferred_element_type=F32)


def block_ranks(owner):
    before = lax.broadcasted_iota(jnp.int32, (PART, PART), 0) < lax.broadcasted_iota(
        jnp.int32, (PART, PART), 1
    )
    before = jnp.where(before, 1.0, 0.0).astype(BF16)
    owned = [jnp.where(owner == device, 1.0, 0.0) for device in range(X * Z)]
    earlier = dot(jnp.concatenate(owned, axis=0).astype(BF16), before)
    blocks = owner.shape[0]
    return sum(
        one * earlier[device * blocks : (device + 1) * blocks] for device, one in enumerate(owned)
    )


def select_kernel(turn_ref, feat_ref, index_ref, out_ref, rank_ref, top_ref, hot_ref):
    rows = feat_ref.shape[1]
    blocks = index_ref.shape[0]
    half = FPAD // 2
    rank = block_ranks(lax.div(index_ref[...], rows))
    rank_ref[...] = rank
    top_ref[0] = jnp.max(rank).astype(jnp.int32)
    first = lax.axis_index("rows") * rows
    skip = (turn_ref[0] * SLOTS).astype(F32)
    slots = lax.broadcasted_iota(jnp.int32, (SLOTS, PART), 0).astype(F32)
    places = lax.broadcasted_iota(jnp.int32, (SLOTS, rows), 1).astype(F32)
    out_ref[...] = jnp.zeros_like(out_ref)

    def find(b, _):
        local = index_ref[pl.ds(b, 1), :] - first
        inside = (local >= 0) & (local < rows)
        chosen = inside & (rank_ref[pl.ds(b, 1), :] - skip == slots)
        place = jnp.sum(jnp.where(chosen, (local + 1).astype(F32), 0.0), axis=1, keepdims=True)
        hot = jnp.where(places == place - 1.0, 1.0, 0.0).astype(BF16)
        hot_ref[pl.ds(pl.multiple_of(b * SLOTS, SLOTS), SLOTS), :] = hot
        return 0

    lax.fori_loop(0, blocks, find, 0, unroll=4)
    for h, stop in ((0, half), (1, FEAT)):
        got = dot_nt(hot_ref[...], feat_ref[h * half : stop, :]).astype(BF16)
        for b in range(blocks):
            to = b // 4 * Z + h * 4 + b % 4
            out_ref[to, :, : stop - h * half] = got[b * SLOTS : (b + 1) * SLOTS]


def place_kernel(turn_ref, in_ref, index_ref, rank_ref, out_ref, *, rows):
    me = lax.axis_index("rows")
    block = pl.ds(lax.div(me, Z) * 4 + lax.rem(me, 4), 1)
    rank = rank_ref[block, :].astype(jnp.int32) - turn_ref[0] * SLOTS
    slot = lax.div(index_ref[block, :], rows) * SLOTS + rank
    slot = jnp.where((rank >= 0) & (rank < SLOTS), slot, -1)
    count = in_ref.shape[0] * SLOTS
    hot = lax.broadcasted_iota(jnp.int32, (count, PART), 0) == slot
    hot = jnp.where(hot, 1.0, 0.0).astype(BF16)
    arrived = in_ref[...].reshape(count, in_ref.shape[2])
    placed = lax.dot_general(
        arrived, hot, (((0,), (0,)), ((), ())), preferred_element_type=F32
    ).astype(BF16)
    for i in range(out_ref.shape[0]):
        out_ref[i] = placed[: FPAD // 2]


def sum_kernel(in_ref, out_ref):
    total = lax.fori_loop(
        0, in_ref.shape[0] // 4,
        lambda i, total: total + sum(in_ref[i * 4 + j].astype(F32) for j in range(4)),
        jnp.zeros(in_ref.shape[1:], F32),
    ).astype(BF16)
    for i in range(out_ref.shape[0]):
        out_ref[i] = total


def split_halves(own_ref, keep_ref, send_ref):
    core = my_core()
    width = keep_ref.shape[1]
    keep_ref[...] = own_ref[:WIRE, pl.ds(pl.multiple_of(core * width, width), width)]
    send_ref[...] = own_ref[:WIRE, pl.ds(pl.multiple_of((1 - core) * width, width), width)]


def own_scores(low_ref, kern_ref, own_ref):
    @pl.loop(0, kern_ref.shape[0] // BLOCK)
    def _(n):
        at = pl.ds(pl.multiple_of(n * BLOCK, BLOCK), BLOCK)
        own_ref[:, at] = dot_nt(low_ref[...], kern_ref[at, :])


def kernel_columns(feat_ref, norm_ref, c_ref, cent_ref, kern_ref, left):
    scale = LOG2E / FEAT
    for z in range(Z):
        height, at = spot(z, FPAD // 2)
        cent_ref[height, at : at + PART] = c_ref[z]
    center_norm = jnp.sum(jnp.square(cent_ref[...].astype(F32)), axis=0, keepdims=True) * scale

    @pl.loop(0, kern_ref.shape[0] // BLOCK)
    def _(n):
        at = pl.ds(pl.multiple_of(n * BLOCK, BLOCK), BLOCK)
        cross = dot(feat_ref[at, :], cent_ref[...])
        power = cross * (2.0 * scale) - center_norm - norm_ref[at, :] * scale
        kern_ref[at, left : left + CHUNK] = jnp.exp2(power).astype(BF16)


def chunk_kernel(feat_ref, norm_ref, c_ref, kern_ref, cent_ref):
    kernel_columns(feat_ref, norm_ref, c_ref, cent_ref, kern_ref, 0)


def build_kernel(
    feat_ref, norm_ref, c_ref, k0, k2, k3, warm_ref,
    kern_ref, coef_ref, own_ref, keep_ref, send_ref, cent_ref, low_ref,
):
    for d, k_ref in ((0, k0), (2, k2), (3, k3)):
        kern_ref[:, d * CHUNK : (d + 1) * CHUNK] = k_ref[...]
    for d in range(X):
        cols = slice(d * CHUNK, (d + 1) * CHUNK)
        warm = warm_ref[:, pl.ds(pl.multiple_of(chunk_of(d) * CHUNK, CHUNK), CHUNK)]
        warm = jnp.concatenate([warm, jnp.zeros((PAD - CLASSES, CHUNK), F32)], axis=0)
        coef_ref[:, cols] = warm
        low_ref[:, cols] = warm.astype(BF16)
    kernel_columns(feat_ref, norm_ref, c_ref, cent_ref, kern_ref, CHUNK)
    own_scores(low_ref, kern_ref, own_ref)
    split_halves(own_ref, keep_ref, send_ref)


def encode_kernel(keep_ref, partner_ref, pair_ref, code_ref):
    pair = keep_ref[...] + partner_ref[...]
    pair_ref[...] = pair
    largest = jnp.max(jnp.abs(pair), axis=0, keepdims=True)
    exponent = jnp.clip(jnp.ceil(jnp.log2(jnp.maximum(largest, 1e-30))), -100.0, 120.0)
    scaled = jnp.floor(pair * jnp.exp2(14.0 - exponent) + 0.5)
    rest = jnp.broadcast_to(exponent, (PAD - WIRE, pair.shape[1]))
    code_ref[...] = jnp.concatenate([scaled, rest], axis=0).astype(jnp.int32).astype(jnp.int16)


def decode_kernel(pair_ref, c0, c1, c2, half_ref):
    total = pair_ref[...]
    for ref in (c0, c1, c2):
        code = ref[...].astype(jnp.int32).astype(F32)
        total = total + code[:WIRE] * jnp.exp2(code[WIRE : WIRE + 1] - 14.0)
    half_ref[...] = total


def add_kernel(keep_ref, partner_ref, *out_refs):
    for d, ref in enumerate(out_refs):
        ref[...] = keep_ref[d] + partner_ref[d]


def residual_of(logits, labels):
    classes = lax.broadcasted_iota(jnp.int32, logits.shape, 0)
    logits = jnp.where(classes < CLASSES, logits, -1e30)
    raised = jnp.exp(logits - jnp.max(logits, axis=0, keepdims=True))
    prob = raised / jnp.sum(raised, axis=0, keepdims=True)
    return (prob - jnp.where(classes == labels, 1.0, 0.0)).astype(BF16)


def gradient_pieces(res_ref, kern_ref, out_ref):
    half = PAD // 2

    @pl.loop(0, X)
    def _(d):
        cols = pl.ds(pl.multiple_of(d * CHUNK, CHUNK), CHUNK)
        grad = dot(res_ref[...], kern_ref[:, cols]).astype(BF16)
        for z in range(Z):
            height, left = spot(z, half)
            out_ref[chunk_of(d) * Z + z] = grad[height, left : left + PART]


def first_kernel(
    mine_ref, theirs_ref, own_ref, kern_ref, label_ref, out_ref, base_ref, res_ref, sum_ref
):
    core = my_core()
    width = mine_ref.shape[1]
    for side, ref in ((core, mine_ref), (1 - core, theirs_ref)):
        sum_ref[:WIRE, pl.ds(pl.multiple_of(side * width, width), width)] = ref[...]
    for n in range(sum_ref.shape[1] // BLOCK):
        at = slice(n * BLOCK, (n + 1) * BLOCK)
        res_ref[:, at] = residual_of(sum_ref[:, at], label_ref[:, at])
    base_ref[...] = sum_ref[...] - own_ref[...]
    gradient_pieces(res_ref, kern_ref, out_ref)


def update(coef_ref, grads, new_ref, low_ref):
    half = PAD // 2

    @pl.loop(0, Z)
    def _(z):
        height = pl.ds(pl.multiple_of(lax.div(z, 4) * half, half), half)
        for d, g_ref in enumerate(grads):
            left = pl.multiple_of(d * CHUNK + lax.rem(z, 4) * PART, PART)
            cols = pl.ds(left, PART)
            fresh = coef_ref[height, cols] - STEP * g_ref[z].astype(F32)
            new_ref[height, cols] = fresh
            low_ref[height, cols] = fresh.astype(BF16)


def second_kernel(coef_ref, g0, g1, g2, g3, base_ref, kern_ref, label_ref, out_ref, new_ref, res_ref, low_ref):
    update(coef_ref, (g0, g1, g2, g3), new_ref, low_ref)

    @pl.loop(0, kern_ref.shape[0] // BLOCK)
    def _(n):
        at = pl.ds(pl.multiple_of(n * BLOCK, BLOCK), BLOCK)
        logits = base_ref[:, at] + dot_nt(low_ref[...], kern_ref[at, :])
        res_ref[:, at] = residual_of(logits, label_ref[:, at])

    gradient_pieces(res_ref, kern_ref, out_ref)


def score_kernel(coef_ref, g0, g1, g2, g3, kern_ref, new_ref, own_ref, keep_ref, send_ref, low_ref):
    update(coef_ref, (g0, g1, g2, g3), new_ref, low_ref)
    own_scores(low_ref, kern_ref, own_ref)
    split_halves(own_ref, keep_ref, send_ref)


def final_kernel(coef_ref, g0, g1, g2, g3, kern_ref, coef_out_ref, keep_ref, send_ref, new_ref, low_ref, own_ref):
    update(coef_ref, (g0, g1, g2, g3), new_ref, low_ref)
    for d in range(X):
        cols = slice(d * CHUNK, (d + 1) * CHUNK)
        to = pl.ds(pl.multiple_of(chunk_of(d) * CHUNK, CHUNK), CHUNK)
        coef_out_ref[:, to] = new_ref[:CLASSES, cols]
    own_scores(low_ref, kern_ref, own_ref)
    core = my_core()
    for d in range(Y):
        y = lax.rem(lax.div(lax.axis_index("centers"), CORES) + d, Y)
        for ref, k in ((keep_ref, core), (send_ref, 1 - core)):
            ref[d] = own_ref[:WIRE, pl.ds(pl.multiple_of((y * CORES + k) * LANES, LANES), LANES)]


def exchange(value, axis, groups=None):
    return lax.all_to_all(
        value, axis, split_axis=0, concat_axis=0, tiled=True, axis_index_groups=groups
    )


def gather(copies):
    mine = exchange(copies, "rows", Z_GROUPS)
    return [mine] + [lax.ppermute(mine, "rows", x_shift(d)) for d in range(1, X)]


def sum_and_gather(pieces):
    arrived = exchange(pieces, "rows")
    copies = call(sum_kernel, like((Z, *pieces.shape[1:]), BF16), name="sum_at_owner")(arrived)
    return gather(copies)


def gather_centers(features, center_index):
    rows = features.shape[1]
    index = center_index.reshape(-1, PART)

    def select(turn):
        return call(
            select_kernel,
            [like((X * Z, SLOTS, 256), BF16), like(index.shape, F32), like((1,), jnp.int32)],
            [pltpu.VMEM((index.shape[0] * SLOTS, rows), BF16)],
            name="select",
            scalars=1,
            last_scalar=True,
        )(turn, features, index)

    def place(turn, pieces, rank):
        return call(
            functools.partial(place_kernel, rows=rows),
            like((Z, FPAD // 2, PART), BF16),
            name="place",
            scalars=1,
        )(turn, exchange(pieces, "rows"), index, rank)

    start = jnp.zeros((1,), jnp.int32)
    pieces, rank, top = select(start)
    copies = place(start, pieces, rank)

    def another(state):
        turn, copies = state
        pieces, rank, _ = select(turn)
        return turn + 1, copies + place(turn, pieces, rank)

    _, copies = lax.while_loop(
        lambda state: state[0][0] * SLOTS <= top[0], another, (start + 1, copies)
    )
    return gather(copies)


def sum_over_groups(keep, send):
    partner = lax.ppermute(send, "centers", CORE_SWAP)
    code_type = like((PAD, keep.shape[1]), jnp.int16)
    pair, code = call(encode_kernel, [like(keep.shape, F32), code_type], name="encode")(
        keep, partner
    )
    codes = [lax.ppermute(code, "centers", y_shift(d)) for d in (2, 1, 3)]
    half = call(decode_kernel, like(keep.shape, F32), name="decode")(pair, *codes)
    return half, lax.ppermute(half, "centers", CORE_SWAP)


def body(features, labels, center_index, warm_coef):
    rows = features.shape[1]
    centers = center_index.shape[1]
    labels = labels.reshape(1, rows)
    kern_type = like((rows, centers), BF16)
    coef_type = like((PAD, centers), F32)
    own_type = like((PAD, rows), F32)
    half_type = like((WIRE, rows // CORES), F32)
    last_type = like((Y, WIRE, LANES), F32)
    grad_type = like((X * Z, PAD // 2, PART), BF16)
    low = pltpu.VMEM((PAD, centers), BF16)
    res = pltpu.VMEM((PAD, rows), BF16)
    score = pltpu.VMEM((PAD, rows), F32)
    coef_scratch = pltpu.VMEM((PAD, centers), F32)

    row_norms = jnp.sum(jnp.square(features.astype(F32)), axis=0).reshape(rows, 1)
    feat_rows = jnp.pad(features, ((0, FPAD - FEAT), (0, 0))).T
    cents = gather_centers(features, center_index)
    build_chunk = call(
        chunk_kernel, like((rows, CHUNK), BF16), [pltpu.VMEM((FPAD, CHUNK), BF16)], name="chunk"
    )
    chunks = [build_chunk(feat_rows, row_norms, cents[d]) for d in (0, 2, 3)]
    kern, coef, own, keep, send = call(
        build_kernel,
        [kern_type, coef_type, own_type, half_type, half_type],
        [pltpu.VMEM((FPAD, CHUNK), BF16), low],
        name="build",
    )(feat_rows, row_norms, cents[1], *chunks, warm_coef)

    for round_idx in range(ROUNDS):
        sums = sum_over_groups(keep, send)
        pieces, base = call(first_kernel, [grad_type, own_type], [res, score], name="first")(
            *sums, own, kern, labels
        )
        for _ in range(1, PASSES):
            grads = sum_and_gather(pieces)
            pieces, coef = call(second_kernel, [grad_type, coef_type], [res, low], name="second")(
                coef, *grads, base, kern, labels
            )
        grads = sum_and_gather(pieces)
        if round_idx < ROUNDS - 1:
            coef, own, keep, send = call(
                score_kernel, [coef_type, own_type, half_type, half_type], [low], name="scores"
            )(coef, *grads, kern)
    coef_out, keep, send = call(
        final_kernel,
        [like((CLASSES, centers), F32), last_type, last_type],
        [coef_scratch, low, score],
        name="final",
    )(coef, *grads, kern)
    partner = lax.ppermute(send, "centers", CORE_SWAP)
    parts = call(add_kernel, [like((WIRE, LANES), F32)] * Y, name="pair")(keep, partner)
    arrived = [lax.ppermute(parts[d], "centers", y_shift(d)) for d in (2, 1, 3)]
    logits_out = (parts[0] + arrived[0] + (arrived[1] + arrived[2]))[:CLASSES]
    return coef_out, logits_out


def solution(mesh):
    return jax.shard_map(
        body,
        mesh=mesh,
        in_specs=(P(None, "rows"), P("rows"), P("centers", None), P(None, "centers")),
        out_specs=(P(None, "centers"), P(None, ("rows", "centers"))),
        check_vma=False,
    )
```

```python
import functools

import jax
import jax.numpy as jnp
from jax import lax
from jax.experimental import pallas as pl
from jax.experimental.pallas import tpu as pltpu
from jax.sharding import PartitionSpec as P

ROUNDS = 2
PASSES = 2
STEP = 0.1

X, Z, Y, CORES = 4, 8, 4, 2
CLASSES = 147
PAD = 160
WIRE = 152
FEAT = 440
FPAD = 448
LANES = 128
CHUNK = X * LANES
PART = CHUNK // 4
BLOCK = 256
SLOTS = 16
EARLY = (0, 3, 2)
GRANT = 20 * 2**20
FLOPS = 2**30

F32 = jnp.float32
BF16 = jnp.bfloat16
LOG2E = 1.4426950408889634

Z_GROUPS = [[x * Z + z for z in range(Z)] for x in range(X)]
CORE_SWAP = [(y * CORES + k, y * CORES + 1 - k) for y in range(Y) for k in range(CORES)]


def x_shift(d):
    return [(x * Z + z, (x + d) % X * Z + z) for x in range(X) for z in range(Z)]


def y_shift(d):
    return [(y * CORES + k, (y + d) % Y * CORES + k) for y in range(Y) for k in range(CORES)]


def call(kernel, outs, scratch=(), name=None, scalars=0, last_scalar=False):
    vmem = pl.BlockSpec(memory_space=pltpu.VMEM)
    smem = pl.BlockSpec(memory_space=pltpu.SMEM)
    many = isinstance(outs, (list, tuple))
    return lambda *args: pl.pallas_call(
        kernel,
        out_shape=outs,
        in_specs=[smem] * scalars + [vmem] * (len(args) - scalars),
        out_specs=([vmem] * (len(outs) - last_scalar) + [smem] * last_scalar) if many else vmem,
        scratch_shapes=list(scratch),
        compiler_params=pltpu.CompilerParams(vmem_limit_bytes=GRANT),
        cost_estimate=pl.CostEstimate(flops=FLOPS, bytes_accessed=2**22, transcendentals=0),
        name=name,
    )(*args)


def like(shape, dtype):
    return jax.ShapeDtypeStruct(shape, dtype)


def my_x():
    return lax.axis_index("rows") // Z


def my_core():
    return lax.rem(lax.axis_index("centers"), CORES)


def chunk_of(d):
    return lax.rem(my_x() + X - d, X)


def spot(z, rows):
    top, left = z // 4 * rows, z % 4 * PART
    return slice(top, top + rows), left


def dot(a, b):
    return jnp.dot(a, b, preferred_element_type=F32)


def dot_nt(a, b):
    return lax.dot_general(a, b, (((1,), (1,)), ((), ())), preferred_element_type=F32)


def block_ranks(owner):
    before = lax.broadcasted_iota(jnp.int32, (PART, PART), 0) < lax.broadcasted_iota(
        jnp.int32, (PART, PART), 1
    )
    before = jnp.where(before, 1.0, 0.0).astype(BF16)
    owned = [jnp.where(owner == device, 1.0, 0.0) for device in range(X * Z)]
    earlier = dot(jnp.concatenate(owned, axis=0).astype(BF16), before)
    blocks = owner.shape[0]
    return sum(
        one * earlier[device * blocks : (device + 1) * blocks] for device, one in enumerate(owned)
    )


def select_kernel(turn_ref, feat_ref, index_ref, out_ref, rank_ref, top_ref, hot_ref):
    rows = feat_ref.shape[1]
    blocks = index_ref.shape[0]
    half = FPAD // 2
    rank = block_ranks(lax.div(index_ref[...], rows))
    rank_ref[...] = rank
    top_ref[0] = jnp.max(rank).astype(jnp.int32)
    first = lax.axis_index("rows") * rows
    skip = (turn_ref[0] * SLOTS).astype(F32)
    slots = lax.broadcasted_iota(jnp.int32, (SLOTS, PART), 0).astype(F32)
    places = lax.broadcasted_iota(jnp.int32, (SLOTS, rows), 1).astype(F32)
    out_ref[...] = jnp.zeros_like(out_ref)

    def find(b, _):
        local = index_ref[pl.ds(b, 1), :] - first
        inside = (local >= 0) & (local < rows)
        chosen = inside & (rank_ref[pl.ds(b, 1), :] - skip == slots)
        place = jnp.sum(jnp.where(chosen, (local + 1).astype(F32), 0.0), axis=1, keepdims=True)
        hot = jnp.where(places == place - 1.0, 1.0, 0.0).astype(BF16)
        hot_ref[pl.ds(pl.multiple_of(b * SLOTS, SLOTS), SLOTS), :] = hot
        return 0

    lax.fori_loop(0, blocks, find, 0, unroll=4)
    for h, stop in ((0, half), (1, FEAT)):
        got = dot_nt(hot_ref[...], feat_ref[h * half : stop, :]).astype(BF16)
        for b in range(blocks):
            to = b // 4 * Z + h * 4 + b % 4
            out_ref[to, :, : stop - h * half] = got[b * SLOTS : (b + 1) * SLOTS]


def place_kernel(turn_ref, in_ref, index_ref, rank_ref, out_ref, *, rows):
    me = lax.axis_index("rows")
    block = pl.ds(lax.div(me, Z) * 4 + lax.rem(me, 4), 1)
    rank = rank_ref[block, :].astype(jnp.int32) - turn_ref[0] * SLOTS
    slot = lax.div(index_ref[block, :], rows) * SLOTS + rank
    slot = jnp.where((rank >= 0) & (rank < SLOTS), slot, -1)
    count = in_ref.shape[0] * SLOTS
    hot = lax.broadcasted_iota(jnp.int32, (count, PART), 0) == slot
    hot = jnp.where(hot, 1.0, 0.0).astype(BF16)
    arrived = in_ref[...].reshape(count, in_ref.shape[2])
    placed = lax.dot_general(
        arrived, hot, (((0,), (0,)), ((), ())), preferred_element_type=F32
    ).astype(BF16)
    for i in range(out_ref.shape[0]):
        out_ref[i] = placed[: FPAD // 2]


def sum_kernel(in_ref, out_ref):
    total = lax.fori_loop(
        0, in_ref.shape[0] // 4,
        lambda i, total: total + sum(in_ref[i * 4 + j].astype(F32) for j in range(4)),
        jnp.zeros(in_ref.shape[1:], F32),
    ).astype(BF16)
    for i in range(out_ref.shape[0]):
        out_ref[i] = total


def split_halves(own_ref, keep_ref, send_ref):
    core = my_core()
    width = keep_ref.shape[1]
    keep_ref[...] = own_ref[:WIRE, pl.ds(pl.multiple_of(core * width, width), width)]
    send_ref[...] = own_ref[:WIRE, pl.ds(pl.multiple_of((1 - core) * width, width), width)]


def add_scores(low_ref, kern_ref, left, before_ref, total_ref):
    @pl.loop(0, kern_ref.shape[0] // BLOCK)
    def _(n):
        at = pl.ds(pl.multiple_of(n * BLOCK, BLOCK), BLOCK)
        scores = dot_nt(low_ref[...], kern_ref[at, left : left + CHUNK])
        total_ref[:, at] = scores if before_ref is None else before_ref[:, at] + scores


def warm_chunk(warm_ref, d, coef_ref, low_ref):
    warm = warm_ref[:, pl.ds(pl.multiple_of(chunk_of(d) * CHUNK, CHUNK), CHUNK)]
    warm = jnp.concatenate([warm, jnp.zeros((PAD - CLASSES, CHUNK), F32)], axis=0)
    coef_ref[...] = warm
    low_ref[...] = warm.astype(BF16)


def kernel_columns(feat_ref, norm_ref, c_ref, cent_ref, kern_ref, left):
    scale = LOG2E / FEAT
    for z in range(Z):
        height, at = spot(z, FPAD // 2)
        cent_ref[height, at : at + PART] = c_ref[z]
    center_norm = jnp.sum(jnp.square(cent_ref[...].astype(F32)), axis=0, keepdims=True) * scale

    @pl.loop(0, kern_ref.shape[0] // BLOCK)
    def _(n):
        at = pl.ds(pl.multiple_of(n * BLOCK, BLOCK), BLOCK)
        cross = dot(feat_ref[at, :], cent_ref[...])
        power = cross * (2.0 * scale) - center_norm - norm_ref[at, :] * scale
        kern_ref[at, left : left + CHUNK] = jnp.exp2(power).astype(BF16)


def chunk_kernel(feat_ref, norm_ref, c_ref, warm_ref, *refs, d):
    before = refs[0] if len(refs) == 6 else None
    kern_ref, coef_ref, total_ref, cent_ref, low_ref = refs[-5:]
    kernel_columns(feat_ref, norm_ref, c_ref, cent_ref, kern_ref, 0)
    warm_chunk(warm_ref, d, coef_ref, low_ref)
    add_scores(low_ref, kern_ref, 0, before, total_ref)


def build_kernel(
    feat_ref, norm_ref, c_ref, warm_ref, before_ref, k0, k2, k3,
    kern_ref, coef_ref, own_ref, keep_ref, send_ref, cent_ref, low_ref,
):
    for d, k_ref in ((0, k0), (2, k2), (3, k3)):
        kern_ref[:, d * CHUNK : (d + 1) * CHUNK] = k_ref[...]
    kernel_columns(feat_ref, norm_ref, c_ref, cent_ref, kern_ref, CHUNK)
    warm_chunk(warm_ref, 1, coef_ref, low_ref)
    add_scores(low_ref, kern_ref, CHUNK, before_ref, own_ref)
    split_halves(own_ref, keep_ref, send_ref)


def encode_kernel(keep_ref, partner_ref, pair_ref, code_ref):
    pair = keep_ref[...] + partner_ref[...]
    pair_ref[...] = pair
    largest = jnp.max(jnp.abs(pair), axis=0, keepdims=True)
    exponent = jnp.clip(jnp.ceil(jnp.log2(jnp.maximum(largest, 1e-30))), -100.0, 120.0)
    scaled = jnp.floor(pair * jnp.exp2(14.0 - exponent) + 0.5)
    rest = jnp.broadcast_to(exponent, (PAD - WIRE, pair.shape[1]))
    code_ref[...] = jnp.concatenate([scaled, rest], axis=0).astype(jnp.int32).astype(jnp.int16)


def decode_kernel(pair_ref, c0, c1, c2, half_ref):
    total = pair_ref[...]
    for ref in (c0, c1, c2):
        code = ref[...].astype(jnp.int32).astype(F32)
        total = total + code[:WIRE] * jnp.exp2(code[WIRE : WIRE + 1] - 14.0)
    half_ref[...] = total


def add_kernel(keep_ref, partner_ref, *out_refs):
    for d, ref in enumerate(out_refs):
        ref[...] = keep_ref[d] + partner_ref[d]


def residual_of(logits, labels):
    classes = lax.broadcasted_iota(jnp.int32, logits.shape, 0)
    logits = jnp.where(classes < CLASSES, logits, -1e30)
    raised = jnp.exp(logits - jnp.max(logits, axis=0, keepdims=True))
    prob = raised / jnp.sum(raised, axis=0, keepdims=True)
    return (prob - jnp.where(classes == labels, 1.0, 0.0)).astype(BF16)


def gradient_pieces(res_ref, kern_ref, out_ref):
    half = PAD // 2

    @pl.loop(0, X)
    def _(d):
        cols = pl.ds(pl.multiple_of(d * CHUNK, CHUNK), CHUNK)
        grad = dot(res_ref[...], kern_ref[:, cols]).astype(BF16)
        for z in range(Z):
            height, left = spot(z, half)
            out_ref[chunk_of(d) * Z + z] = grad[height, left : left + PART]


def first_kernel(
    mine_ref, theirs_ref, own_ref, kern_ref, label_ref, out_ref, base_ref, res_ref, sum_ref
):
    core = my_core()
    width = mine_ref.shape[1]
    for side, ref in ((core, mine_ref), (1 - core, theirs_ref)):
        sum_ref[:WIRE, pl.ds(pl.multiple_of(side * width, width), width)] = ref[...]
    for n in range(sum_ref.shape[1] // BLOCK):
        at = slice(n * BLOCK, (n + 1) * BLOCK)
        res_ref[:, at] = residual_of(sum_ref[:, at], label_ref[:, at])
    base_ref[...] = sum_ref[...] - own_ref[...]
    gradient_pieces(res_ref, kern_ref, out_ref)


def update(coef_ref, g_ref, new_ref, low_ref):
    half = PAD // 2

    @pl.loop(0, Z)
    def _(z):
        height = pl.ds(pl.multiple_of(lax.div(z, 4) * half, half), half)
        cols = pl.ds(pl.multiple_of(lax.rem(z, 4) * PART, PART), PART)
        fresh = coef_ref[height, cols] - STEP * g_ref[z].astype(F32)
        new_ref[height, cols] = fresh
        low_ref[height, cols] = fresh.astype(BF16)


def step_kernel(coef_ref, g_ref, kern_ref, *refs, d):
    before = refs[0] if len(refs) == 4 else None
    new_ref, total_ref, low_ref = refs[-3:]
    update(coef_ref, g_ref, new_ref, low_ref)
    add_scores(low_ref, kern_ref, d * CHUNK, before, total_ref)


def second_kernel(
    coef_ref, g_ref, before_ref, base_ref, kern_ref, label_ref, out_ref, new_ref, res_ref, low_ref
):
    update(coef_ref, g_ref, new_ref, low_ref)

    @pl.loop(0, kern_ref.shape[0] // BLOCK)
    def _(n):
        at = pl.ds(pl.multiple_of(n * BLOCK, BLOCK), BLOCK)
        last = dot_nt(low_ref[...], kern_ref[at, CHUNK : 2 * CHUNK])
        logits = base_ref[:, at] + (before_ref[:, at] + last)
        res_ref[:, at] = residual_of(logits, label_ref[:, at])

    gradient_pieces(res_ref, kern_ref, out_ref)


def score_kernel(
    coef_ref, g_ref, before_ref, kern_ref, new_ref, own_ref, keep_ref, send_ref, low_ref
):
    update(coef_ref, g_ref, new_ref, low_ref)
    add_scores(low_ref, kern_ref, CHUNK, before_ref, own_ref)
    split_halves(own_ref, keep_ref, send_ref)


def final_kernel(
    c0, c2, c3, coef_ref, g_ref, before_ref, kern_ref,
    coef_out_ref, keep_ref, send_ref, new_ref, low_ref, own_ref,
):
    update(coef_ref, g_ref, new_ref, low_ref)
    for d, ref in enumerate((c0, new_ref, c2, c3)):
        to = pl.ds(pl.multiple_of(chunk_of(d) * CHUNK, CHUNK), CHUNK)
        coef_out_ref[:, to] = ref[:CLASSES, :]
    add_scores(low_ref, kern_ref, CHUNK, before_ref, own_ref)
    core = my_core()
    for d in range(Y):
        y = lax.rem(lax.div(lax.axis_index("centers"), CORES) + d, Y)
        for ref, k in ((keep_ref, core), (send_ref, 1 - core)):
            ref[d] = own_ref[:WIRE, pl.ds(pl.multiple_of((y * CORES + k) * LANES, LANES), LANES)]


def exchange(value, axis, groups=None):
    return lax.all_to_all(
        value, axis, split_axis=0, concat_axis=0, tiled=True, axis_index_groups=groups
    )


def gather(copies):
    mine = exchange(copies, "rows", Z_GROUPS)
    return [mine] + [lax.ppermute(mine, "rows", x_shift(d)) for d in range(1, X)]


def sum_and_gather(pieces):
    arrived = exchange(pieces, "rows")
    copies = call(sum_kernel, like((Z, *pieces.shape[1:]), BF16), name="sum_at_owner")(arrived)
    return gather(copies)


def gather_centers(features, center_index):
    rows = features.shape[1]
    index = center_index.reshape(-1, PART)

    def select(turn):
        return call(
            select_kernel,
            [like((X * Z, SLOTS, 256), BF16), like(index.shape, F32), like((1,), jnp.int32)],
            [pltpu.VMEM((index.shape[0] * SLOTS, rows), BF16)],
            name="select",
            scalars=1,
            last_scalar=True,
        )(turn, features, index)

    def place(turn, pieces, rank):
        return call(
            functools.partial(place_kernel, rows=rows),
            like((Z, FPAD // 2, PART), BF16),
            name="place",
            scalars=1,
        )(turn, exchange(pieces, "rows"), index, rank)

    start = jnp.zeros((1,), jnp.int32)
    pieces, rank, top = select(start)
    copies = place(start, pieces, rank)

    def another(state):
        turn, copies = state
        pieces, rank, _ = select(turn)
        return turn + 1, copies + place(turn, pieces, rank)

    _, copies = lax.while_loop(
        lambda state: state[0][0] * SLOTS <= top[0], another, (start + 1, copies)
    )
    return gather(copies)


def sum_over_groups(keep, send):
    partner = lax.ppermute(send, "centers", CORE_SWAP)
    code_type = like((PAD, keep.shape[1]), jnp.int16)
    pair, code = call(encode_kernel, [like(keep.shape, F32), code_type], name="encode")(
        keep, partner
    )
    codes = [lax.ppermute(code, "centers", y_shift(d)) for d in (2, 1, 3)]
    half = call(decode_kernel, like(keep.shape, F32), name="decode")(pair, *codes)
    return half, lax.ppermute(half, "centers", CORE_SWAP)


def body(features, labels, center_index, warm_coef):
    rows = features.shape[1]
    centers = center_index.shape[1]
    labels = labels.reshape(1, rows)
    kern_type = like((rows, centers), BF16)
    coef_type = like((PAD, CHUNK), F32)
    own_type = like((PAD, rows), F32)
    half_type = like((WIRE, rows // CORES), F32)
    last_type = like((Y, WIRE, LANES), F32)
    grad_type = like((X * Z, PAD // 2, PART), BF16)
    low = pltpu.VMEM((PAD, CHUNK), BF16)
    res = pltpu.VMEM((PAD, rows), BF16)
    score = pltpu.VMEM((PAD, rows), F32)
    cent = pltpu.VMEM((FPAD, CHUNK), BF16)

    row_norms = jnp.sum(jnp.square(features.astype(F32)), axis=0).reshape(rows, 1)
    feat_rows = jnp.pad(features, ((0, FPAD - FEAT), (0, 0))).T
    cents = gather_centers(features, center_index)
    before, chunks, coefs = [], {}, {}
    for d in EARLY:
        chunks[d], coefs[d], total = call(
            functools.partial(chunk_kernel, d=d),
            [like((rows, CHUNK), BF16), coef_type, own_type],
            [cent, low],
            name="chunk",
        )(feat_rows, row_norms, cents[d], warm_coef, *before)
        before = [total]
    kern, coefs[1], own, keep, send = call(
        build_kernel,
        [kern_type, coef_type, own_type, half_type, half_type],
        [cent, low],
        name="build",
    )(feat_rows, row_norms, cents[1], warm_coef, *before, chunks[0], chunks[2], chunks[3])

    def early_steps(coefs, grads):
        coefs, before = dict(coefs), []
        for d in EARLY:
            coefs[d], total = call(
                functools.partial(step_kernel, d=d), [coef_type, own_type], [low], name="step"
            )(coefs[d], grads[d], kern, *before)
            before = [total]
        return coefs, before[0]

    for round_idx in range(ROUNDS):
        mine, theirs = sum_over_groups(keep, send)
        pieces, base = call(first_kernel, [grad_type, own_type], [res, score], name="first")(
            mine, theirs, own, kern, labels
        )
        for _ in range(1, PASSES):
            grads = sum_and_gather(pieces)
            coefs, total = early_steps(coefs, grads)
            pieces, coefs[1] = call(
                second_kernel, [grad_type, coef_type], [res, low], name="second"
            )(coefs[1], grads[1], total, base, kern, labels)
        grads = sum_and_gather(pieces)
        coefs, total = early_steps(coefs, grads)
        if round_idx < ROUNDS - 1:
            coefs[1], own, keep, send = call(
                score_kernel, [coef_type, own_type, half_type, half_type], [low], name="scores"
            )(coefs[1], grads[1], total, kern)
    coef_out, keep, send = call(
        final_kernel,
        [like((CLASSES, centers), F32), last_type, last_type],
        [pltpu.VMEM((PAD, CHUNK), F32), low, score],
        name="final",
    )(coefs[0], coefs[2], coefs[3], coefs[1], grads[1], total, kern)
    partner = lax.ppermute(send, "centers", CORE_SWAP)
    parts = call(add_kernel, [like((WIRE, LANES), F32)] * Y, name="pair")(keep, partner)
    arrived = [lax.ppermute(parts[d], "centers", y_shift(d)) for d in (2, 1, 3)]
    logits_out = (parts[0] + arrived[0] + (arrived[1] + arrived[2]))[:CLASSES]
    return coef_out, logits_out


def solution(mesh):
    return jax.shard_map(
        body,
        mesh=mesh,
        in_specs=(P(None, "rows"), P("rows"), P("centers", None), P(None, "centers")),
        out_specs=(P(None, "centers"), P(None, ("rows", "centers"))),
        check_vma=False,
    )
```

```python
import functools

import jax
import jax.numpy as jnp
from jax import lax
from jax.experimental import pallas as pl
from jax.experimental.pallas import tpu as pltpu
from jax.sharding import PartitionSpec as P

ROUNDS = 2
PASSES = 2
STEP = 0.1

X, Z, Y, CORES = 4, 8, 4, 2
CLASSES = 147
PAD = 160
WIRE = 152
FEAT = 440
FPAD = 448
LANES = 128
CHUNK = X * LANES
PART = CHUNK // 4
BLOCK = 256
SLOTS = 16
EARLY = (0, 3, 2)
GRANT = 20 * 2**20
FLOPS = 2**30

F32 = jnp.float32
BF16 = jnp.bfloat16
LOG2E = 1.4426950408889634

Z_GROUPS = [[x * Z + z for z in range(Z)] for x in range(X)]
CORE_SWAP = [(y * CORES + k, y * CORES + 1 - k) for y in range(Y) for k in range(CORES)]


def x_shift(d):
    return [(x * Z + z, (x + d) % X * Z + z) for x in range(X) for z in range(Z)]


def y_shift(d):
    return [(y * CORES + k, (y + d) % Y * CORES + k) for y in range(Y) for k in range(CORES)]


def call(kernel, outs, scratch=(), name=None, scalars=0, far=0, last_scalar=False):
    vmem = pl.BlockSpec(memory_space=pltpu.VMEM)
    smem = pl.BlockSpec(memory_space=pltpu.SMEM)
    many = isinstance(outs, (list, tuple))
    return lambda *args: pl.pallas_call(
        kernel,
        out_shape=outs,
        in_specs=[smem] * scalars
        + [vmem] * (len(args) - scalars - far)
        + [pl.BlockSpec(memory_space=pltpu.HBM)] * far,
        out_specs=([vmem] * (len(outs) - last_scalar) + [smem] * last_scalar) if many else vmem,
        scratch_shapes=list(scratch),
        compiler_params=pltpu.CompilerParams(vmem_limit_bytes=GRANT),
        cost_estimate=pl.CostEstimate(flops=FLOPS, bytes_accessed=2**22, transcendentals=0),
        name=name,
    )(*args)


def like(shape, dtype):
    return jax.ShapeDtypeStruct(shape, dtype)


def my_x():
    return lax.axis_index("rows") // Z


def my_core():
    return lax.rem(lax.axis_index("centers"), CORES)


def chunk_of(d):
    return lax.rem(my_x() + X - d, X)


def spot(z, rows):
    top, left = z // 4 * rows, z % 4 * PART
    return slice(top, top + rows), left


def dot(a, b):
    return jnp.dot(a, b, preferred_element_type=F32)


def dot_nt(a, b):
    return lax.dot_general(a, b, (((1,), (1,)), ((), ())), preferred_element_type=F32)


def block_ranks(owner):
    before = lax.broadcasted_iota(jnp.int32, (PART, PART), 0) < lax.broadcasted_iota(
        jnp.int32, (PART, PART), 1
    )
    before = jnp.where(before, 1.0, 0.0).astype(BF16)
    owned = [jnp.where(owner == device, 1.0, 0.0) for device in range(X * Z)]
    earlier = dot(jnp.concatenate(owned, axis=0).astype(BF16), before)
    blocks = owner.shape[0]
    return sum(
        one * earlier[device * blocks : (device + 1) * blocks] for device, one in enumerate(owned)
    )


def select_kernel(
    turn_ref, index_ref, far_ref, out_ref, rank_ref, top_ref, hot_ref, feat_ref, copied
):
    copy = pltpu.make_async_copy(far_ref, feat_ref, copied)
    copy.start()
    rows = feat_ref.shape[1]
    blocks = index_ref.shape[0]
    half = FPAD // 2
    rank = block_ranks(lax.div(index_ref[...], rows))
    rank_ref[...] = rank
    top_ref[0] = jnp.max(rank).astype(jnp.int32)
    first = lax.axis_index("rows") * rows
    skip = (turn_ref[0] * SLOTS).astype(F32)
    slots = lax.broadcasted_iota(jnp.int32, (SLOTS, PART), 0).astype(F32)
    places = lax.broadcasted_iota(jnp.int32, (SLOTS, rows), 1).astype(F32)
    out_ref[...] = jnp.zeros_like(out_ref)

    def find(b, _):
        local = index_ref[pl.ds(b, 1), :] - first
        inside = (local >= 0) & (local < rows)
        chosen = inside & (rank_ref[pl.ds(b, 1), :] - skip == slots)
        place = jnp.sum(jnp.where(chosen, (local + 1).astype(F32), 0.0), axis=1, keepdims=True)
        hot = jnp.where(places == place - 1.0, 1.0, 0.0).astype(BF16)
        hot_ref[pl.ds(pl.multiple_of(b * SLOTS, SLOTS), SLOTS), :] = hot
        return 0

    lax.fori_loop(0, blocks, find, 0, unroll=4)
    copy.wait()
    for h, stop in ((0, half), (1, FEAT)):
        got = dot_nt(hot_ref[...], feat_ref[h * half : stop, :]).astype(BF16)
        for b in range(blocks):
            to = b // 4 * Z + h * 4 + b % 4
            out_ref[to, :, : stop - h * half] = got[b * SLOTS : (b + 1) * SLOTS]


def place_kernel(turn_ref, in_ref, index_ref, rank_ref, out_ref, *, rows):
    me = lax.axis_index("rows")
    block = pl.ds(lax.div(me, Z) * 4 + lax.rem(me, 4), 1)
    rank = rank_ref[block, :].astype(jnp.int32) - turn_ref[0] * SLOTS
    slot = lax.div(index_ref[block, :], rows) * SLOTS + rank
    slot = jnp.where((rank >= 0) & (rank < SLOTS), slot, -1)
    count = in_ref.shape[0] * SLOTS
    hot = lax.broadcasted_iota(jnp.int32, (count, PART), 0) == slot
    hot = jnp.where(hot, 1.0, 0.0).astype(BF16)
    arrived = in_ref[...].reshape(count, in_ref.shape[2])
    placed = lax.dot_general(
        arrived, hot, (((0,), (0,)), ((), ())), preferred_element_type=F32
    ).astype(BF16)
    for i in range(out_ref.shape[0]):
        out_ref[i] = placed[: FPAD // 2]


def sum_kernel(in_ref, out_ref):
    total = lax.fori_loop(
        0, in_ref.shape[0] // 4,
        lambda i, total: total + sum(in_ref[i * 4 + j].astype(F32) for j in range(4)),
        jnp.zeros(in_ref.shape[1:], F32),
    ).astype(BF16)
    for i in range(out_ref.shape[0]):
        out_ref[i] = total


def split_halves(own_ref, keep_ref, send_ref):
    core = my_core()
    width = keep_ref.shape[1]
    keep_ref[...] = own_ref[:WIRE, pl.ds(pl.multiple_of(core * width, width), width)]
    send_ref[...] = own_ref[:WIRE, pl.ds(pl.multiple_of((1 - core) * width, width), width)]


def add_scores(low_ref, kern_ref, left, before_ref, total_ref):
    @pl.loop(0, kern_ref.shape[0] // BLOCK)
    def _(n):
        at = pl.ds(pl.multiple_of(n * BLOCK, BLOCK), BLOCK)
        scores = dot_nt(low_ref[...], kern_ref[at, left : left + CHUNK])
        total_ref[:, at] = scores if before_ref is None else before_ref[:, at] + scores


def warm_chunk(warm_ref, d, coef_ref, low_ref):
    warm = warm_ref[:, pl.ds(pl.multiple_of(chunk_of(d) * CHUNK, CHUNK), CHUNK)]
    warm = jnp.concatenate([warm, jnp.zeros((PAD - CLASSES, CHUNK), F32)], axis=0)
    coef_ref[...] = warm
    low_ref[...] = warm.astype(BF16)


def kernel_columns(feat_ref, norm_ref, c_ref, cent_ref, kern_ref, left):
    scale = LOG2E / FEAT
    for z in range(Z):
        height, at = spot(z, FPAD // 2)
        cent_ref[height, at : at + PART] = c_ref[z]
    center_norm = jnp.sum(jnp.square(cent_ref[...].astype(F32)), axis=0, keepdims=True) * scale

    @pl.loop(0, kern_ref.shape[0] // BLOCK)
    def _(n):
        at = pl.ds(pl.multiple_of(n * BLOCK, BLOCK), BLOCK)
        cross = dot(feat_ref[at, :], cent_ref[...])
        power = cross * (2.0 * scale) - center_norm - norm_ref[at, :] * scale
        kern_ref[at, left : left + CHUNK] = jnp.exp2(power).astype(BF16)


def chunk_kernel(feat_ref, norm_ref, c_ref, warm_ref, *refs, d):
    before = refs[0] if len(refs) == 6 else None
    kern_ref, coef_ref, total_ref, cent_ref, low_ref = refs[-5:]
    kernel_columns(feat_ref, norm_ref, c_ref, cent_ref, kern_ref, 0)
    warm_chunk(warm_ref, d, coef_ref, low_ref)
    add_scores(low_ref, kern_ref, 0, before, total_ref)


def build_kernel(
    feat_ref, norm_ref, c_ref, warm_ref, before_ref, k0, k2, k3,
    kern_ref, coef_ref, own_ref, keep_ref, send_ref, cent_ref, low_ref,
):
    for d, k_ref in ((0, k0), (2, k2), (3, k3)):
        kern_ref[:, d * CHUNK : (d + 1) * CHUNK] = k_ref[...]
    kernel_columns(feat_ref, norm_ref, c_ref, cent_ref, kern_ref, CHUNK)
    warm_chunk(warm_ref, 1, coef_ref, low_ref)
    add_scores(low_ref, kern_ref, CHUNK, before_ref, own_ref)
    split_halves(own_ref, keep_ref, send_ref)


def encode_kernel(keep_ref, partner_ref, pair_ref, code_ref):
    pair = keep_ref[...] + partner_ref[...]
    pair_ref[...] = pair
    largest = jnp.max(jnp.abs(pair), axis=0, keepdims=True)
    exponent = jnp.clip(jnp.ceil(jnp.log2(jnp.maximum(largest, 1e-30))), -100.0, 120.0)
    scaled = jnp.floor(pair * jnp.exp2(14.0 - exponent) + 0.5)
    rest = jnp.broadcast_to(exponent, (PAD - WIRE, pair.shape[1]))
    code_ref[...] = jnp.concatenate([scaled, rest], axis=0).astype(jnp.int32).astype(jnp.int16)


def decode_kernel(pair_ref, c0, c1, c2, half_ref):
    total = pair_ref[...]
    for ref in (c0, c1, c2):
        code = ref[...].astype(jnp.int32).astype(F32)
        total = total + code[:WIRE] * jnp.exp2(code[WIRE : WIRE + 1] - 14.0)
    half_ref[...] = total


def add_kernel(keep_ref, partner_ref, *out_refs):
    for d, ref in enumerate(out_refs):
        ref[...] = keep_ref[d] + partner_ref[d]


def residual_of(logits, labels):
    classes = lax.broadcasted_iota(jnp.int32, logits.shape, 0)
    logits = jnp.where(classes < CLASSES, logits, -1e30)
    raised = jnp.exp(logits - jnp.max(logits, axis=0, keepdims=True))
    prob = raised / jnp.sum(raised, axis=0, keepdims=True)
    return (prob - jnp.where(classes == labels, 1.0, 0.0)).astype(BF16)


def gradient_pieces(res_ref, kern_ref, out_ref):
    half = PAD // 2

    @pl.loop(0, X)
    def _(d):
        cols = pl.ds(pl.multiple_of(d * CHUNK, CHUNK), CHUNK)
        grad = dot(res_ref[...], kern_ref[:, cols]).astype(BF16)
        for z in range(Z):
            height, left = spot(z, half)
            out_ref[chunk_of(d) * Z + z] = grad[height, left : left + PART]


def first_kernel(
    mine_ref, theirs_ref, own_ref, kern_ref, label_ref, out_ref, base_ref, res_ref, sum_ref
):
    core = my_core()
    width = mine_ref.shape[1]
    for side, ref in ((core, mine_ref), (1 - core, theirs_ref)):
        sum_ref[:WIRE, pl.ds(pl.multiple_of(side * width, width), width)] = ref[...]
    for n in range(sum_ref.shape[1] // BLOCK):
        at = slice(n * BLOCK, (n + 1) * BLOCK)
        res_ref[:, at] = residual_of(sum_ref[:, at], label_ref[:, at])
    base_ref[...] = sum_ref[...] - own_ref[...]
    gradient_pieces(res_ref, kern_ref, out_ref)


def update(coef_ref, g_ref, new_ref, low_ref):
    half = PAD // 2

    @pl.loop(0, Z)
    def _(z):
        height = pl.ds(pl.multiple_of(lax.div(z, 4) * half, half), half)
        cols = pl.ds(pl.multiple_of(lax.rem(z, 4) * PART, PART), PART)
        fresh = coef_ref[height, cols] - STEP * g_ref[z].astype(F32)
        new_ref[height, cols] = fresh
        low_ref[height, cols] = fresh.astype(BF16)


def step_kernel(coef_ref, g_ref, kern_ref, *refs, d):
    before = refs[0] if len(refs) == 4 else None
    new_ref, total_ref, low_ref = refs[-3:]
    update(coef_ref, g_ref, new_ref, low_ref)
    add_scores(low_ref, kern_ref, d * CHUNK, before, total_ref)


def second_kernel(
    coef_ref, g_ref, before_ref, base_ref, kern_ref, label_ref, out_ref, new_ref, res_ref, low_ref
):
    update(coef_ref, g_ref, new_ref, low_ref)

    @pl.loop(0, kern_ref.shape[0] // BLOCK)
    def _(n):
        at = pl.ds(pl.multiple_of(n * BLOCK, BLOCK), BLOCK)
        last = dot_nt(low_ref[...], kern_ref[at, CHUNK : 2 * CHUNK])
        logits = base_ref[:, at] + (before_ref[:, at] + last)
        res_ref[:, at] = residual_of(logits, label_ref[:, at])

    gradient_pieces(res_ref, kern_ref, out_ref)


def score_kernel(
    coef_ref, g_ref, before_ref, kern_ref, new_ref, own_ref, keep_ref, send_ref, low_ref
):
    update(coef_ref, g_ref, new_ref, low_ref)
    add_scores(low_ref, kern_ref, CHUNK, before_ref, own_ref)
    split_halves(own_ref, keep_ref, send_ref)


def final_kernel(
    coef_ref, g_ref, before_ref, kern_ref, new_ref, keep_ref, send_ref, low_ref, own_ref
):
    update(coef_ref, g_ref, new_ref, low_ref)
    add_scores(low_ref, kern_ref, CHUNK, before_ref, own_ref)
    core = my_core()
    for d in range(Y):
        y = lax.rem(lax.div(lax.axis_index("centers"), CORES) + d, Y)
        for ref, k in ((keep_ref, core), (send_ref, 1 - core)):
            ref[d] = own_ref[:WIRE, pl.ds(pl.multiple_of((y * CORES + k) * LANES, LANES), LANES)]


def order_kernel(c0, c1, c2, c3, coef_out_ref):
    for d, ref in enumerate((c0, c1, c2, c3)):
        to = pl.ds(pl.multiple_of(chunk_of(d) * CHUNK, CHUNK), CHUNK)
        coef_out_ref[:, to] = ref[:CLASSES, :]


def exchange(value, axis, groups=None):
    return lax.all_to_all(
        value, axis, split_axis=0, concat_axis=0, tiled=True, axis_index_groups=groups
    )


def gather(copies):
    mine = exchange(copies, "rows", Z_GROUPS)
    return [mine] + [lax.ppermute(mine, "rows", x_shift(d)) for d in range(1, X)]


def sum_and_gather(pieces):
    arrived = exchange(pieces, "rows")
    copies = call(sum_kernel, like((Z, *pieces.shape[1:]), BF16), name="sum_at_owner")(arrived)
    return gather(copies)


def gather_centers(features, center_index, beside):
    rows = features.shape[1]
    index = center_index.reshape(-1, PART)

    def select(turn):
        return call(
            select_kernel,
            [like((X * Z, SLOTS, 256), BF16), like(index.shape, F32), like((1,), jnp.int32)],
            [
                pltpu.VMEM((index.shape[0] * SLOTS, rows), BF16),
                pltpu.VMEM(features.shape, BF16),
                pltpu.SemaphoreType.DMA,
            ],
            name="select",
            scalars=1,
            far=1,
            last_scalar=True,
        )(turn, index, features)

    def place(turn, pieces, rank):
        return call(
            functools.partial(place_kernel, rows=rows),
            like((Z, FPAD // 2, PART), BF16),
            name="place",
            scalars=1,
        )(turn, exchange(pieces, "rows"), index, rank)

    start = jnp.zeros((1,), jnp.int32)
    pieces, rank, top = select(start)
    copies = place(start, pieces, rank)
    copies, beside = lax.optimization_barrier((copies, beside))

    def another(state):
        turn, copies = state
        pieces, rank, _ = select(turn)
        return turn + 1, copies + place(turn, pieces, rank)

    _, copies = lax.while_loop(
        lambda state: state[0][0] * SLOTS <= top[0], another, (start + 1, copies)
    )
    return gather(copies), beside


def sum_over_groups(keep, send):
    partner = lax.ppermute(send, "centers", CORE_SWAP)
    code_type = like((PAD, keep.shape[1]), jnp.int16)
    pair, code = call(encode_kernel, [like(keep.shape, F32), code_type], name="encode")(
        keep, partner
    )
    codes = [lax.ppermute(code, "centers", y_shift(d)) for d in (2, 1, 3)]
    half = call(decode_kernel, like(keep.shape, F32), name="decode")(pair, *codes)
    return half, lax.ppermute(half, "centers", CORE_SWAP)


def body(features, labels, center_index, warm_coef):
    rows = features.shape[1]
    centers = center_index.shape[1]
    labels = labels.reshape(1, rows)
    kern_type = like((rows, centers), BF16)
    coef_type = like((PAD, CHUNK), F32)
    own_type = like((PAD, rows), F32)
    half_type = like((WIRE, rows // CORES), F32)
    last_type = like((Y, WIRE, LANES), F32)
    grad_type = like((X * Z, PAD // 2, PART), BF16)
    low = pltpu.VMEM((PAD, CHUNK), BF16)
    res = pltpu.VMEM((PAD, rows), BF16)
    score = pltpu.VMEM((PAD, rows), F32)
    cent = pltpu.VMEM((FPAD, CHUNK), BF16)

    row_norms = jnp.sum(jnp.square(features.astype(F32)), axis=0).reshape(rows, 1)
    feat_rows = jnp.pad(features, ((0, FPAD - FEAT), (0, 0))).T
    cents, (feat_rows, row_norms) = gather_centers(
        features, center_index, (feat_rows, row_norms)
    )
    before, chunks, coefs = [], {}, {}
    for d in EARLY:
        chunks[d], coefs[d], total = call(
            functools.partial(chunk_kernel, d=d),
            [like((rows, CHUNK), BF16), coef_type, own_type],
            [cent, low],
            name="chunk",
        )(feat_rows, row_norms, cents[d], warm_coef, *before)
        before = [total]
    kern, coefs[1], own, keep, send = call(
        build_kernel,
        [kern_type, coef_type, own_type, half_type, half_type],
        [cent, low],
        name="build",
    )(feat_rows, row_norms, cents[1], warm_coef, *before, chunks[0], chunks[2], chunks[3])

    def early_steps(coefs, grads):
        coefs, before = dict(coefs), []
        for d in EARLY:
            coefs[d], total = call(
                functools.partial(step_kernel, d=d), [coef_type, own_type], [low], name="step"
            )(coefs[d], grads[d], kern, *before)
            before = [total]
        return coefs, before[0]

    for round_idx in range(ROUNDS):
        mine, theirs = sum_over_groups(keep, send)
        pieces, base = call(first_kernel, [grad_type, own_type], [res, score], name="first")(
            mine, theirs, own, kern, labels
        )
        for _ in range(1, PASSES):
            grads = sum_and_gather(pieces)
            coefs, total = early_steps(coefs, grads)
            pieces, coefs[1] = call(
                second_kernel, [grad_type, coef_type], [res, low], name="second"
            )(coefs[1], grads[1], total, base, kern, labels)
        grads = sum_and_gather(pieces)
        coefs, total = early_steps(coefs, grads)
        if round_idx < ROUNDS - 1:
            coefs[1], own, keep, send = call(
                score_kernel, [coef_type, own_type, half_type, half_type], [low], name="scores"
            )(coefs[1], grads[1], total, kern)
    coefs[1], keep, send = call(
        final_kernel, [coef_type, last_type, last_type], [low, score], name="final"
    )(coefs[1], grads[1], total, kern)
    coef_out = call(order_kernel, like((CLASSES, centers), F32), name="order")(
        *(coefs[d] for d in range(X))
    )
    partner = lax.ppermute(send, "centers", CORE_SWAP)
    parts = call(add_kernel, [like((WIRE, LANES), F32)] * Y, name="pair")(keep, partner)
    arrived = [lax.ppermute(parts[d], "centers", y_shift(d)) for d in (2, 1, 3)]
    logits_out = (parts[0] + arrived[0] + (arrived[1] + arrived[2]))[:CLASSES]
    return coef_out, logits_out


def solution(mesh):
    return jax.shard_map(
        body,
        mesh=mesh,
        in_specs=(P(None, "rows"), P("rows"), P("centers", None), P(None, "centers")),
        out_specs=(P(None, "centers"), P(None, ("rows", "centers"))),
        check_vma=False,
    )
```
